32 devices in a mesh: mem: 8 (over y, x, core), st: 4 (over z).
Axes of the slice: x: 2, y: 2, z: 4, core: 2. Of those that a mesh axis runs over, the one named last changes fastest.
Arguments:
- ensemble: float32 [8192, 256], P('st', 'mem'), may hold values from -8 to 8
- obs_values: float32 [4, 8, 128], replicated, may hold values from -8 to 8
- obs_sigma: float32 [4, 8, 128], replicated, may hold values from 0.25 to 0.5
- obs_operator: float32 [4, 8, 2, 128, 128], replicated, may hold values from -0.375 to 0.375
- block_cols: int32 [4, 8, 2], replicated, may hold values from 0 to 63
- batch_order: int32 [4], replicated, may hold values from 0 to 3, each once
Outputs:
- analysis: float32 [8192, 256], P('st', 'mem')
- log_weights: float32 [256], P('mem')
- ess: float32 [], replicated
The draws below stay inside these ranges and needn't reach their ends.
Inputs may be any that keep to these rules, and one draw needn't show every extreme that they name: `block_cols`: block indices of the whole state. `batch_order`: each batch exactly once.
All inputs are finite; a program needn't handle non-finite values.
Results may differ from the reference program's by a relative error of at most 0.0003.
Values sent between devices are 32-bit elements; how exact they have to be, the bound alone decides.
A program may use at most 64 MiB of HBM per device.

```python
import math
import jax
import jax.numpy as jnp
from jax import lax

SBLK = 128
OB = 8
KB = 2
NBATCH = 4
MEMBERS = 256
NBLK = 64
STATE = 8192
NOBS = 4096


mode_count = 64


def draw_ensemble(key, part):
    base_key = jax.random.fold_in(key, 11)
    load_key = jax.random.fold_in(key, 12)
    series_key = jax.random.fold_in(key, 13)
    base = jax.random.normal(base_key, (STATE, MEMBERS), jnp.float32)
    loadings = jax.random.normal(load_key, (STATE, mode_count), jnp.float32)
    series = jax.random.normal(series_key, (mode_count, MEMBERS), jnp.float32)
    amplitude = jnp.exp2(-jnp.arange(mode_count, dtype=jnp.float32) / 6.0)

    def add_mode(index, total):
        column = lax.dynamic_index_in_dim(loadings, index, 1, keepdims=False)
        row = lax.dynamic_index_in_dim(series, index, 0, keepdims=False)
        scale = lax.dynamic_index_in_dim(amplitude, index, 0, keepdims=False)
        return total + scale * column[:, None] * row[None, :]
    total = lax.fori_loop(0, mode_count, add_mode, 0.5 * base)
    return jnp.clip(total, -8.0, 8.0).astype(jnp.float32)


def touch_ends(entries, own_key, least, high):
    longest = entries.shape.index(max(entries.shape))
    spots = []
    for shift in (0, 1):
        where = [jax.random.randint(jax.random.fold_in(own_key, axis), (), 0, length) for axis, length in enumerate(entries.shape)]
        where[longest] = (where[longest] + shift) % entries.shape[longest]
        spots.append(tuple(where))
    return entries.at[spots[0]].set(least).at[spots[1]].set(high)


def centred(stream_key, extent, spread, limit, kind=jnp.bfloat16):
    drawn = spread * jax.random.normal(stream_key, extent, jnp.float32)
    return jnp.clip(drawn, min=-limit, max=limit).astype(kind)


def setup_inputs(seed: int = 0) -> dict:
    seeds = jax.random.split(jax.random.key(seed), 7)
    ensemble = draw_ensemble(jax.random.fold_in(seeds[6], 71), 0)
    obs_values = centred(seeds[1], (NBATCH, OB, SBLK), 1.5, 8.0, jnp.float32)
    obs_sigma = jnp.clip(jnp.exp(jax.random.uniform(seeds[2], (NBATCH, OB, SBLK), jnp.float32, math.log(0.25), math.log(0.5))), 0.25, 0.5)
    obs_operator = centred(seeds[3], (NBATCH, OB, KB, SBLK, SBLK), (KB * SBLK) ** -0.5, 0.375, jnp.float32)
    block_cols = touch_ends(jax.random.randint(seeds[4], (NBATCH, OB, KB), 0, NBLK), jax.random.fold_in(seeds[4], 1), 0, NBLK - 1).astype(jnp.int32)
    batch_order = jax.random.permutation(seeds[5], NBATCH).astype(jnp.int32)
    return dict(ensemble=ensemble, obs_values=obs_values, obs_sigma=obs_sigma, obs_operator=obs_operator, block_cols=block_cols, batch_order=batch_order)


precise = lax.Precision.HIGHEST

def solve_blocks(moment, target):
    factor = jnp.linalg.cholesky(moment)
    return jax.vmap(lambda lower, right: jax.scipy.linalg.cho_solve((lower, True), right))(factor, target)

def reference(ensemble, obs_values, obs_sigma, obs_operator, block_cols, batch_order):
    states = ensemble.reshape(NBLK, SBLK, MEMBERS)
    loglik = jnp.zeros((MEMBERS,), jnp.float32)
    temper = 1.0 / math.sqrt(NOBS)
    eye = jnp.eye(SBLK, dtype=jnp.float32)
    for batch_step in range(NBATCH):
        chosen = batch_order[batch_step]
        operator_now = obs_operator[chosen]
        columns = block_cols[chosen].astype(jnp.int32)
        values_now = obs_values[chosen]
        sigma_now = obs_sigma[chosen]
        picked = states[columns]
        image = jnp.einsum('bkij,bkjm->bim', operator_now, picked, precision=precise)
        center = lax.optimization_barrier(jnp.sum(image, axis=2)) / MEMBERS
        anomaly = image - center[:, :, None]
        misfit = (values_now[:, :, None] - image) / sigma_now[:, :, None]
        loglik = loglik - 0.5 * temper * lax.optimization_barrier(jnp.sum(misfit * misfit, axis=(0, 1)))
        moment = jnp.einsum('bim,bjm->bij', anomaly, anomaly, precision=precise) / (MEMBERS - 1)
        moment = moment + eye * (sigma_now * sigma_now)[:, :, None]
        cross = jnp.einsum('bkim,bjm->bkij', picked, anomaly, precision=precise) / (MEMBERS - 1)
        target = (values_now - center)[:, :, None] - 0.5 * anomaly
        weights = solve_blocks(moment, target)
        change = jnp.einsum('bkij,bjm->bkim', cross, weights, precision=precise)
        states = states.at[columns.reshape(-1)].add(change.reshape(-1, SBLK, MEMBERS))
    largest = jnp.max(loglik)
    scaled = jnp.exp(loglik - largest)
    summed = jnp.sum(scaled)
    squares = jnp.sum(scaled * scaled)
    log_weights = loglik - largest - jnp.log(summed)
    ess = summed * summed / squares
    return (states.reshape(STATE, MEMBERS), log_weights, ess)
```

```python
import functools
import math

import jax
import jax.numpy as jnp
from jax import lax
from jax.experimental import pallas as pl
from jax.experimental.pallas import tpu as pltpu
from jax.sharding import PartitionSpec as P

precise = lax.Precision.HIGHEST
PANEL = 16
GATHER_LIMIT = 16 << 20


def halves(x):
    high = x.astype(jnp.bfloat16)
    return high, (x - high.astype(jnp.float32)).astype(jnp.bfloat16)


def thirds(x):
    high = x.astype(jnp.bfloat16)
    rest = x - high.astype(jnp.float32)
    mid = rest.astype(jnp.bfloat16)
    return high, mid, (rest - mid.astype(jnp.float32)).astype(jnp.bfloat16)


def mul_nn(a, b):
    return lax.dot_general(a, b, (((1,), (0,)), ((), ())), preferred_element_type=jnp.float32)


def mul_nt(a, b):
    return lax.dot_general(a, b, (((1,), (1,)), ((), ())), preferred_element_type=jnp.float32)


def factor_panel(moments, pivots, obs_blocks, size, first):
    lanes = lax.broadcasted_iota(jnp.int32, (obs_blocks, size), 1)
    inside = (lanes >= first) & (lanes < first + PANEL)
    entry, rows = {}, []
    for i in range(PANEL):
        row = moments[pl.ds(first + i, obs_blocks, stride=size), :]
        for j in range(i + 1):
            entry[i, j] = jnp.broadcast_to(row[:, first + j : first + j + 1], (obs_blocks, size))
        rows.append(jnp.where(inside, (lanes == first + i).astype(jnp.float32), row))
    for p in range(PANEL):
        pivot = entry[p, p]
        root = lax.rsqrt(pivot)
        root = root * (1.5 - 0.5 * pivot * root * root)
        rows[p] = rows[p] * root
        column = {i: entry[i, p] * root for i in range(p + 1, PANEL)}
        for i in range(p + 1, PANEL):
            for j in range(p + 1, i + 1):
                entry[i, j] = entry[i, j] - column[i] * column[j]
        for i in range(p + 1, PANEL):
            rows[i] = rows[i] - column[i] * rows[p]
    for i in range(PANEL):
        pivots[pl.ds(i, obs_blocks, stride=PANEL), :] = rows[i]
    for b in range(obs_blocks):
        moments[b * size + first : b * size + first + PANEL, :] = pivots[b * PANEL : (b + 1) * PANEL, :]
    below = first + PANEL
    if below == size:
        return
    stack = pivots[...]
    across = stack.T[below:, :]
    depth = obs_blocks * PANEL
    half = depth // 2
    high, mid, low = thirds(stack)
    left = [jnp.concatenate([x[:half], jnp.zeros((half, size), x.dtype)], axis=0) for x in (high, mid, low)]
    right = [jnp.concatenate([jnp.zeros((half, size), x.dtype), x[half:]], axis=0) for x in (high, mid, low)]
    both = [jnp.concatenate(x, axis=1) for x in zip(left, right)]
    rhs = jnp.concatenate([both[0], both[1], both[0], both[1], both[0], both[2]], axis=0)
    high, mid, low = thirds(across)
    wide = jnp.concatenate([high, high, mid, mid, low, high], axis=1)
    pair = (lax.broadcasted_iota(jnp.int32, (1, depth), 1) % half) // PANEL
    cols = lax.broadcasted_iota(jnp.int32, (size - below, size), 1)
    in_panel = (cols >= first) & (cols < below)
    for g in range(obs_blocks // 2):
        mask = (pair == g).astype(jnp.float32).astype(jnp.bfloat16)
        product = mul_nn(wide * jnp.concatenate([mask] * 6, axis=1), rhs)
        for b, update in ((g, product[:, :size]), (g + obs_blocks // 2, product[:, size:])):
            old = moments[b * size + below : (b + 1) * size, :]
            moments[b * size + below : (b + 1) * size, :] = jnp.where(in_panel, 0.0, old) - update


def kernel(
    members, order, columns, place, values, sigma, operator, gathered,
    analysis, logw, ess,
    states, operators, picks, parts, moments, pivots, misfits, sems, operator_sems,
):
    batches, obs_blocks, size = values.shape
    groups, width, _ = gathered.shape
    mem_count = members // width
    blocks = gathered.shape[2] // size
    fetches = [
        pltpu.make_async_copy(operator.at[order[t]], operators.at[t], operator_sems.at[t])
        for t in range(batches)
    ]
    copies = []
    for g in range(groups):
        z, m = g // mem_count, g % mem_count
        copies.append(
            pltpu.make_async_copy(
                gathered.at[g], states.at[z, pl.ds(m * width, width), :], sems.at[g]
            )
        )
    for copy in copies:
        copy.start()
    for fetch in fetches:
        fetch.start()
    misfits[...] = jnp.zeros_like(misfits)
    for copy in copies:
        copy.wait()
    for fetch in fetches:
        fetch.wait()
    line = lax.broadcasted_iota(jnp.int32, (size, size), 0)
    cols = lax.broadcasted_iota(jnp.int32, (size, size), 1)
    eye = (line == cols).astype(jnp.float32)
    below_diagonal = line >= cols

    def spot(block):
        return block // blocks, pl.ds(pl.multiple_of((block % blocks) * size, size), size)

    @pl.loop(0, batches)
    def _(step):
        chosen = order[step]
        values_now, sigma_now = values[chosen], sigma[chosen]
        values_t, sigma_t = values_now.T, sigma_now.T
        centers = []
        for b in range(obs_blocks):
            sides = []
            for k in range(2):
                z, lane = spot(columns[chosen, k, b])
                sides.append(states[z, :, lane])
            high, mid = halves(jnp.concatenate(sides, axis=1))
            picks[b, 0] = high
            picks[b, 1] = mid
            h_high, h_mid = halves(jnp.concatenate([operators[step, b, 0], operators[step, b, 1]], axis=1))
            image = mul_nt(jnp.concatenate([h_high, h_mid], axis=0), high)
            image = image[:size] + image[size:] + mul_nt(h_high, mid)
            value, deviation = values_t[:, b : b + 1], sigma_t[:, b : b + 1]
            misfit = (value - image) * (1.0 / deviation)
            misfits[...] += jnp.sum((misfit * misfit).reshape(size // 8, 8, members), axis=0)
            center = jnp.sum(image, axis=1, keepdims=True) * (1.0 / members)
            centers.append(center)
            high, mid, low = thirds(image - center)
            tall = jnp.concatenate([high, mid, low], axis=0)
            parts[b] = tall
            product = mul_nt(tall, tall[: 2 * size])
            total = (product[size : 2 * size, size:] + product[2 * size :, :size]) + mul_nt(high, low)
            total = (product[:size, size:] + product[size : 2 * size, :size] + total) + product[:size, :size]
            moments[b * size : (b + 1) * size, :] = total * (1.0 / (members - 1)) + eye * (deviation * deviation)
        offsets = values_now - jnp.concatenate(centers, axis=1).T

        for panel in range(size // PANEL):
            factor_panel(moments, pivots, obs_blocks, size, panel * PANEL)

        for b in range(obs_blocks):
            lower = jnp.where(below_diagonal, moments[b * size : (b + 1) * size, :], 0.0)
            shift = jnp.sum(lower * offsets[b : b + 1, :], axis=1, keepdims=True)
            l_high, l_mid, l_low = thirds(lower)
            tall = parts[b]
            pair = jnp.concatenate([jnp.concatenate([l_high, l_high], axis=1), jnp.concatenate([l_mid, l_mid], axis=1)], axis=0)
            first = mul_nn(pair, tall[: 2 * size])
            last = mul_nn(jnp.concatenate([l_low, l_high], axis=1), jnp.concatenate([tall[:size], tall[2 * size :]], axis=0))
            whitened = first[:size] + (first[size:] + last)
            target = (shift - 0.5 * whitened).T * (1.0 / (members - 1))
            y_high, y_mid = halves(whitened)
            cross = mul_nn(jnp.concatenate([y_high, y_mid], axis=0), picks[b, 0])
            cross = cross[:size] + cross[size:] + mul_nn(y_high, picks[b, 1])
            c_high, c_mid = halves(cross)
            t_high, t_mid = halves(target)
            change = mul_nn(jnp.concatenate([t_high, t_high], axis=1), jnp.concatenate([c_high, c_mid], axis=0))
            change = change + mul_nn(t_mid, c_high)
            for k in range(2):
                z, lane = spot(columns[chosen, k, b])
                states[z, :, lane] += change[:, k * size : (k + 1) * size]

    temper = 1.0 / math.sqrt(batches * obs_blocks * size)
    likely = -0.5 * temper * jnp.sum(misfits[...], axis=0, keepdims=True)
    largest = jnp.max(likely, axis=1, keepdims=True)
    scaled = jnp.exp(likely - largest)
    summed = jnp.sum(scaled, axis=1, keepdims=True)
    squares = jnp.sum(scaled * scaled, axis=1, keepdims=True)
    ess[...] = summed * summed / squares
    logs = jnp.broadcast_to(likely - largest - jnp.log(summed), (8, members))
    logs = pltpu.roll(logs, lax.rem(members - place[0] * width, members), 1)
    logw[...] = logs[:1, :width]
    analysis[...] = states[place[1], pl.ds(pl.multiple_of(place[0] * width, width), width), :]


MESH = pl.DeviceIdType.MESH


def gather_kernel(piece, gathered, send_sems, recv_sems, local_sem):
    me, z = lax.axis_index("mem"), lax.axis_index("st")
    depth, width = lax.axis_size("st"), lax.axis_size("mem")
    core, bit = me % 2, (me // 2) % 2
    twin = me + 1 - 2 * core
    flat = me + 2 - 4 * bit
    upright = (me + width // 2) % width
    corner = (flat + width // 2) % width
    kinds = {"up": 0, "down": 1, "flat": 2, "upright": 3, "twin": 4}
    targets = {"up": (me, z + 1), "down": (me, z - 1), "flat": (flat, z), "upright": (upright, z), "twin": (twin, z)}

    def copy(kind, slot, source=None):
        return pltpu.make_async_remote_copy(
            src_ref=gathered.at[slot] if source is None else source,
            dst_ref=gathered.at[slot],
            send_sem=send_sems.at[kinds[kind] * depth * width + slot],
            recv_sem=recv_sems.at[slot],
            device_id=targets[kind],
            device_id_type=MESH,
        )

    def arrive(slot):
        copy("twin", slot).wait_recv()

    barrier = pltpu.get_barrier_semaphore()
    for kind in ("flat", "upright", "twin"):
        pl.semaphore_signal(barrier, inc=1, device_id=targets[kind], device_id_type=MESH)

    @pl.when(z < depth - 1)
    def _():
        pl.semaphore_signal(barrier, inc=1, device_id=targets["up"], device_id_type=MESH)

    @pl.when(z > 0)
    def _():
        pl.semaphore_signal(barrier, inc=1, device_id=targets["down"], device_id_type=MESH)

    @pl.when((z > 0) & (z < depth - 1))
    def _():
        pl.semaphore_wait(barrier, 5)

    @pl.when((z == 0) | (z == depth - 1))
    def _():
        pl.semaphore_wait(barrier, 4)

    def column(action, level, distance, rising):
        slot = level * width + me
        source = piece if distance == 0 else None
        if distance == 0 or rising:
            @pl.when(z < depth - 1)
            def _():
                action(copy("up", slot, source))

        if distance == 0 or not rising:
            @pl.when(z > 0)
            def _():
                action(copy("down", slot, source))

        for kind in ("flat", "upright", "twin"):
            action(copy(kind, slot, source))

    def plane(action, level, wait):
        for first, onward, parity in ((flat, "upright", 1), (upright, "flat", 0)):
            slot = level * width + first
            if wait:
                arrive(slot)

            @pl.when(level % 2 == parity)
            def _():
                action(copy(onward, slot))

            action(copy("twin", slot))

    def far(action, level, wait):
        slot = level * width + corner
        if wait:
            arrive(slot)
        action(copy("twin", slot))

    def around(distance, do):
        if distance == 0:
            do(z, True)
            return

        @pl.when(z >= distance)
        def _():
            do(z - distance, True)

        @pl.when(z + distance < depth)
        def _():
            do(z + distance, False)

    def start(descriptor):
        descriptor.start()

    def finish(descriptor):
        descriptor.wait_send()

    own = pltpu.make_async_copy(piece, gathered.at[z * width + me], local_sem)
    own.start()
    column(start, z, 0, True)

    for turn in range(1, depth + 2):
        if turn < depth:
            def onward(level, rising, turn=turn):
                arrive(level * width + me)
                column(start, level, turn, rising)
            around(turn, onward)
        if turn - 1 < depth:
            around(turn - 1, lambda level, rising: plane(start, level, True))
        if turn >= 2:
            around(turn - 2, lambda level, rising: far(start, level, True))
    for distance in range(depth):
        def rest(level, rising, distance=distance):
            for other in (twin, flat + twin - me, upright + twin - me, corner + twin - me):
                arrive(level * width + other)
            column(finish, level, distance, rising)
            plane(finish, level, False)
            far(finish, level, False)
        around(distance, rest)
    own.wait()


def gather_all(piece):
    depth, width = lax.axis_size("st"), lax.axis_size("mem")
    if width != 8 or depth < 2:
        return lax.all_gather(piece, ("st", "mem"))
    anywhere = pl.BlockSpec(memory_space=pl.ANY)
    return pl.pallas_call(
        gather_kernel,
        out_shape=jax.ShapeDtypeStruct((depth * width, *piece.shape), piece.dtype),
        in_specs=[anywhere],
        out_specs=anywhere,
        scratch_shapes=[
            pltpu.SemaphoreType.DMA((5 * depth * width,)),
            pltpu.SemaphoreType.DMA((depth * width,)),
            pltpu.SemaphoreType.DMA,
        ],
        compiler_params=pltpu.CompilerParams(collective_id=0, has_side_effects=True),
    )(piece)


def gathered_shards(ensemble, obs_values, obs_sigma, obs_operator, block_cols, batch_order):
    size = obs_operator.shape[-1]
    row_count, width = ensemble.shape
    blocks = row_count // size
    mem_count, st_count = lax.axis_size("mem"), lax.axis_size("st")
    members = width * mem_count
    batches, obs_blocks, _ = block_cols.shape
    gathered = gather_all(ensemble.T)
    place = jnp.stack([lax.axis_index("mem"), lax.axis_index("st")]).astype(jnp.int32)
    smem = pl.BlockSpec(memory_space=pltpu.SMEM)
    vmem = pl.BlockSpec(memory_space=pltpu.VMEM)
    anywhere = pl.BlockSpec(memory_space=pl.ANY)
    analysis, logw, ess = pl.pallas_call(
        functools.partial(kernel, members),
        out_shape=(
            jax.ShapeDtypeStruct((width, row_count), jnp.float32),
            jax.ShapeDtypeStruct((1, width), jnp.float32),
            jax.ShapeDtypeStruct((1, 1), jnp.float32),
        ),
        in_specs=[smem, smem, smem, vmem, vmem, anywhere, anywhere],
        out_specs=(vmem, vmem, vmem),
        scratch_shapes=[
            pltpu.VMEM((st_count, members, row_count), jnp.float32),
            pltpu.VMEM(obs_operator.shape, jnp.float32),
            pltpu.VMEM((obs_blocks, 2, members, 2 * size), jnp.bfloat16),
            pltpu.VMEM((obs_blocks, 3 * size, members), jnp.bfloat16),
            pltpu.VMEM((size * obs_blocks, size), jnp.float32),
            pltpu.VMEM((PANEL * obs_blocks, size), jnp.float32),
            pltpu.VMEM((8, members), jnp.float32),
            pltpu.SemaphoreType.DMA((mem_count * st_count,)),
            pltpu.SemaphoreType.DMA((batches,)),
        ],
        compiler_params=pltpu.CompilerParams(vmem_limit_bytes=48 << 20),
    )(batch_order, block_cols.transpose(0, 2, 1), place, obs_values, obs_sigma, obs_operator, gathered)
    return analysis.T, logw.reshape(width), ess.reshape(())


def solve_blocks(moment, target):
    factor = jnp.linalg.cholesky(moment)
    return jax.vmap(lambda lower, right: jax.scipy.linalg.cho_solve((lower, True), right))(
        factor, target
    )


def reduced_shards(ensemble, obs_values, obs_sigma, obs_operator, block_cols, batch_order):
    block_size = obs_operator.shape[-1]
    row_count, mem_dev = ensemble.shape
    nblocks = row_count // block_size
    members = mem_dev * lax.axis_size("mem")
    batches, obs_blocks, col_count = block_cols.shape
    temper = 1.0 / math.sqrt(batches * obs_blocks * block_size)
    offset = lax.axis_index("st") * nblocks
    states = ensemble.reshape(nblocks, block_size, mem_dev)
    eye = jnp.eye(block_size, dtype=jnp.float32)
    slots = jnp.arange(nblocks, dtype=jnp.int32)
    loglik = jnp.zeros((mem_dev,), jnp.float32)
    for batch_step in range(batches):
        chosen = batch_order[batch_step]
        operator_now = lax.dynamic_index_in_dim(obs_operator, chosen, 0, keepdims=False)
        columns = lax.dynamic_index_in_dim(block_cols, chosen, 0, keepdims=False)
        values_now = lax.dynamic_index_in_dim(obs_values, chosen, 0, keepdims=False)
        sigma_now = lax.dynamic_index_in_dim(obs_sigma, chosen, 0, keepdims=False)
        local_ids = columns.reshape(-1) - offset
        selector = (local_ids[:, None] == slots[None, :]).astype(jnp.float32)
        picked = jnp.einsum("ps,sim->pim", selector, states, precision=precise)
        picked = picked.reshape(obs_blocks, col_count, block_size, mem_dev)
        partial_value = jnp.einsum("bkij,bkjm->bim", operator_now, picked, precision=precise)
        image = lax.psum(partial_value, "st")
        misfit = (values_now[:, :, None] - image) / sigma_now[:, :, None]
        loglik = loglik - 0.5 * temper * jnp.sum(misfit * misfit, axis=(0, 1))
        center = lax.psum(jnp.sum(image, axis=2), "mem") / members
        anomaly = image - center[:, :, None]
        moment_sum, cross_sum = lax.psum(
            (
                jnp.einsum("bim,bjm->bij", anomaly, anomaly, precision=precise),
                jnp.einsum("bkim,bjm->bkij", picked, anomaly, precision=precise),
            ),
            "mem",
        )
        moment = moment_sum / (members - 1) + eye * (sigma_now * sigma_now)[:, :, None]
        cross = cross_sum / (members - 1)
        target = (values_now - center)[:, :, None] - 0.5 * anomaly
        weights = solve_blocks(moment, target)
        change = jnp.einsum("bkij,bjm->bkim", cross, weights, precision=precise)
        change = change.reshape(obs_blocks * col_count, block_size, mem_dev)
        states = states + jnp.einsum("ps,pim->sim", selector, change, precision=precise)
    largest_local = jnp.max(loglik)
    largest = lax.pmax(largest_local, "mem")
    scaled = jnp.exp(loglik - largest)
    summed, squares = lax.psum((jnp.sum(scaled), jnp.sum(scaled * scaled)), "mem")
    log_weights = loglik - largest - jnp.log(summed)
    ess = summed * summed / squares
    return (states.reshape(row_count, mem_dev), log_weights, ess)


def shards(ensemble, *others):
    devices = lax.axis_size("mem") * lax.axis_size("st")
    fits = 4 * ensemble.size * devices <= GATHER_LIMIT
    return (gathered_shards if fits else reduced_shards)(ensemble, *others)


def solution(mesh):
    placed = (P("st", "mem"), P(), P(), P(), P(), P())
    return jax.shard_map(
        shards,
        mesh=mesh,
        in_specs=placed,
        out_specs=(P("st", "mem"), P("mem"), P()),
        check_vma=False,
    )
```

```python
import functools
import math

import jax
import jax.numpy as jnp
from jax import lax
from jax.experimental import pallas as pl
from jax.experimental.pallas import tpu as pltpu
from jax.sharding import PartitionSpec as P

precise = lax.Precision.HIGHEST
PANEL = 16
SUB = 8
GATHER_LIMIT = 16 << 20


def halves(x):
    high = x.astype(jnp.bfloat16)
    return high, (x - high.astype(jnp.float32)).astype(jnp.bfloat16)


def thirds(x):
    high = x.astype(jnp.bfloat16)
    rest = x - high.astype(jnp.float32)
    mid = rest.astype(jnp.bfloat16)
    return high, mid, (rest - mid.astype(jnp.float32)).astype(jnp.bfloat16)


def mul_nn(a, b):
    return lax.dot_general(a, b, (((1,), (0,)), ((), ())), preferred_element_type=jnp.float32)


def mul_nt(a, b):
    return lax.dot_general(a, b, (((1,), (1,)), ((), ())), preferred_element_type=jnp.float32)


def factor(moments, crossed, obs_blocks, size):
    lanes = lax.broadcasted_iota(jnp.int32, (obs_blocks, size), 1)
    own = lanes % obs_blocks == lax.broadcasted_iota(jnp.int32, (obs_blocks, size), 0)
    own = own.astype(jnp.float32)[:, : PANEL * obs_blocks]

    def spread(rows, lane):
        count = len(rows)
        tall = jnp.concatenate(rows, axis=0)
        tall = jnp.broadcast_to(tall[:, lane : lane + 1], (count * obs_blocks, size))
        return [tall[r * obs_blocks : (r + 1) * obs_blocks] for r in range(count)]

    def line(r):
        return slice(r * obs_blocks, (r + 1) * obs_blocks)

    def updates(rhs, low, high):
        parts = []
        for k in range(3):
            wide = [jnp.broadcast_to(crossed[k, r : r + 1, :], own.shape) * own for r in range(low, high)]
            parts.append(jnp.concatenate(wide, axis=0).astype(jnp.bfloat16))
        main = mul_nn(jnp.concatenate([parts[0], parts[1]], axis=1), rhs[0])
        return main[:, size:] + mul_nn(jnp.concatenate([parts[2], parts[0]], axis=1), rhs[1]) + main[:, :size]

    rows = [moments[line(i), :] for i in range(PANEL)]
    for first in range(0, size, PANEL):
        for sub in range(0, PANEL, SUB):
            base = first + sub
            inside = (lanes >= base) & (lanes < base + SUB)
            entry = {}
            for j in range(SUB):
                for i, value in zip(range(j, SUB), spread(rows[sub + j : sub + SUB], base + j)):
                    entry[i, j] = value
            for i in range(SUB):
                rows[sub + i] = jnp.where(inside, (lanes == base + i).astype(jnp.float32), rows[sub + i])
            for p in range(SUB):
                root = lax.rsqrt(entry[p, p])
                rows[sub + p] = rows[sub + p] * root
                column = {i: entry[i, p] * root for i in range(p + 1, SUB)}
                for i in range(p + 1, SUB):
                    for j in range(p + 1, i + 1):
                        entry[i, j] = entry[i, j] - column[i] * column[j]
                for i in range(p + 1, SUB):
                    rows[sub + i] = rows[sub + i] - column[i] * rows[sub + p]
            for i in range(sub + SUB, PANEL):
                row = jnp.where(inside, 0.0, rows[i])
                for p, value in zip(range(sub, sub + SUB), spread(rows[sub : sub + SUB], first + i)):
                    row = row - value * rows[p]
                rows[i] = row
        for i in range(PANEL - SUB):
            later = first + i // SUB * SUB + SUB
            rows[i] = jnp.where((lanes >= later) & (lanes < first + PANEL), 0.0, rows[i])
        for i in range(PANEL):
            moments[line(first + i), :] = rows[i]
        below = first + PANEL
        if below == size:
            return
        stack = jnp.concatenate(rows, axis=0)
        high, mid, low = thirds(stack)
        across = thirds(stack.T)
        for k in range(3):
            crossed[k, :, :] = across[k].astype(jnp.float32)
        rhs = [
            jnp.concatenate([jnp.concatenate([high, mid], axis=1)] * 2, axis=0),
            jnp.concatenate([high, low], axis=0),
        ]
        inside = (lanes >= first) & (lanes < below)
        change = updates(rhs, below, below + PANEL)
        rows = [jnp.where(inside, 0.0, moments[line(below + i), :]) - change[line(i)] for i in range(PANEL)]
        if below + PANEL < size:
            change = updates(rhs, below + PANEL, size)
            for i in range(size - below - PANEL):
                here = line(below + PANEL + i)
                moments[here, :] = jnp.where(inside, 0.0, moments[here, :]) - change[line(i)]


def kernel(
    members, order, columns, place, values, sigma, operator, gathered,
    states, analysis, logw, ess,
    picks, parts, moments, crossed, misfits, whites, targets, crosses,
):
    batches, obs_blocks, size = values.shape
    _, width, row_count = states.shape
    mem_count = members // width
    blocks = row_count // size
    misfits[...] = jnp.zeros_like(misfits)
    line = lax.broadcasted_iota(jnp.int32, (size, size), 0)
    cols = lax.broadcasted_iota(jnp.int32, (size, size), 1)
    eye = (line == cols).astype(jnp.float32)
    below_diagonal = line >= cols

    def spot(block):
        level = pl.ds((block // blocks) * mem_count, mem_count)
        return level, slice(None), pl.ds(pl.multiple_of((block % blocks) * size, size), size)

    @pl.loop(0, batches)
    def _(step):
        chosen = order[step]
        values_now, sigma_now = values[chosen], sigma[chosen]
        values_t, sigma_t = values_now.T, sigma_now.T
        centers = []
        for b in range(obs_blocks):
            sides = []
            for k in range(2):
                sides.append(states[spot(columns[chosen, k, b])].reshape(members, size))
            high, mid = halves(jnp.concatenate(sides, axis=1))
            picks[b, 0] = high
            picks[b, 1] = mid
            h_high, h_mid = halves(jnp.concatenate([operator[chosen, b, 0], operator[chosen, b, 1]], axis=1))
            image = mul_nt(jnp.concatenate([h_high, h_mid], axis=0), high)
            image = image[:size] + image[size:] + mul_nt(h_high, mid)
            value, deviation = values_t[:, b : b + 1], sigma_t[:, b : b + 1]
            misfit = (value - image) * (1.0 / deviation)
            misfits[...] += jnp.sum((misfit * misfit).reshape(size // 8, 8, members), axis=0)
            center = jnp.sum(image, axis=1, keepdims=True) * (1.0 / members)
            centers.append(center)
            high, mid, low = thirds(image - center)
            tall = jnp.concatenate([high, mid, low], axis=0)
            parts[b] = tall
        for b in range(obs_blocks):
            tall = parts[b]
            high, low = tall[:size], tall[2 * size :]
            deviation = sigma_t[:, b : b + 1]
            product = mul_nt(tall, tall[: 2 * size])
            total = (product[size : 2 * size, size:] + product[2 * size :, :size]) + mul_nt(high, low)
            total = (product[:size, size:] + product[size : 2 * size, :size] + total) + product[:size, :size]
            moments[pl.ds(b, size, stride=obs_blocks), :] = total * (1.0 / (members - 1)) + eye * (deviation * deviation)
        offsets = values_now - jnp.concatenate(centers, axis=1).T

        factor(moments, crossed, obs_blocks, size)

        for b in range(obs_blocks):
            lower = jnp.where(below_diagonal, moments[pl.ds(b, size, stride=obs_blocks), :], 0.0)
            shift = jnp.sum(lower * offsets[b : b + 1, :], axis=1, keepdims=True)
            l_high, l_mid, l_low = thirds(lower)
            tall = parts[b]
            pair = jnp.concatenate([jnp.concatenate([l_high, l_high], axis=1), jnp.concatenate([l_mid, l_mid], axis=1)], axis=0)
            first = mul_nn(pair, tall[: 2 * size])
            last = mul_nn(jnp.concatenate([l_low, l_high], axis=1), jnp.concatenate([tall[:size], tall[2 * size :]], axis=0))
            whitened = first[:size] + (first[size:] + last)
            whites[b] = jnp.concatenate(halves(whitened), axis=0)
            targets[b] = (shift - 0.5 * whitened) * (1.0 / (members - 1))
        for b in range(obs_blocks):
            cross = mul_nn(whites[b], picks[b, 0])
            cross = cross[:size] + cross[size:] + mul_nn(whites[b, :size], picks[b, 1])
            crosses[b] = jnp.concatenate(halves(cross), axis=0)
        for b in range(obs_blocks):
            t_high, t_mid = halves(targets[b].T)
            change = mul_nn(jnp.concatenate([t_high, t_high], axis=1), crosses[b])
            change = change + mul_nn(t_mid, crosses[b, :size])
            for k in range(2):
                where = spot(columns[chosen, k, b])
                states[where] += change[:, k * size : (k + 1) * size].reshape(mem_count, width, size)

    temper = 1.0 / math.sqrt(batches * obs_blocks * size)
    likely = -0.5 * temper * jnp.sum(misfits[...], axis=0, keepdims=True)
    largest = jnp.max(likely, axis=1, keepdims=True)
    scaled = jnp.exp(likely - largest)
    summed = jnp.sum(scaled, axis=1, keepdims=True)
    squares = jnp.sum(scaled * scaled, axis=1, keepdims=True)
    ess[...] = summed * summed / squares
    logs = jnp.broadcast_to(likely - largest - jnp.log(summed), (8, members))
    logs = pltpu.roll(logs, lax.rem(members - place[0] * width, members), 1)
    logw[...] = logs[:1, :width]
    analysis[...] = states[place[1] * mem_count + place[0]]


MESH = pl.DeviceIdType.MESH


def gather_kernel(piece, gathered, send_sems, recv_sems, local_sem):
    me, z = lax.axis_index("mem"), lax.axis_index("st")
    depth, width = lax.axis_size("st"), lax.axis_size("mem")
    core, bit = me % 2, (me // 2) % 2
    twin = me + 1 - 2 * core
    flat = me + 2 - 4 * bit
    upright = (me + width // 2) % width
    corner = (flat + width // 2) % width
    kinds = {"up": 0, "down": 1, "flat": 2, "upright": 3, "twin": 4}
    targets = {"up": (me, z + 1), "down": (me, z - 1), "flat": (flat, z), "upright": (upright, z), "twin": (twin, z)}

    def copy(kind, slot, source=None):
        return pltpu.make_async_remote_copy(
            src_ref=gathered.at[slot] if source is None else source,
            dst_ref=gathered.at[slot],
            send_sem=send_sems.at[kinds[kind] * depth * width + slot],
            recv_sem=recv_sems.at[slot],
            device_id=targets[kind],
            device_id_type=MESH,
        )

    def arrive(slot):
        copy("twin", slot).wait_recv()

    barrier = pltpu.get_barrier_semaphore()
    for kind in ("flat", "upright", "twin"):
        pl.semaphore_signal(barrier, inc=1, device_id=targets[kind], device_id_type=MESH)

    @pl.when(z < depth - 1)
    def _():
        pl.semaphore_signal(barrier, inc=1, device_id=targets["up"], device_id_type=MESH)

    @pl.when(z > 0)
    def _():
        pl.semaphore_signal(barrier, inc=1, device_id=targets["down"], device_id_type=MESH)

    @pl.when((z > 0) & (z < depth - 1))
    def _():
        pl.semaphore_wait(barrier, 5)

    @pl.when((z == 0) | (z == depth - 1))
    def _():
        pl.semaphore_wait(barrier, 4)

    def column(action, level, distance, rising):
        slot = level * width + me
        source = piece if distance == 0 else None
        if distance == 0 or rising:
            @pl.when(z < depth - 1)
            def _():
                action(copy("up", slot, source))

        if distance == 0 or not rising:
            @pl.when(z > 0)
            def _():
                action(copy("down", slot, source))

        for kind in ("flat", "upright", "twin"):
            action(copy(kind, slot, source))

    def plane(action, level, wait):
        for first, onward, parity in ((flat, "upright", 1), (upright, "flat", 0)):
            slot = level * width + first
            if wait:
                arrive(slot)

            @pl.when(level % 2 == parity)
            def _():
                action(copy(onward, slot))

            action(copy("twin", slot))

    def far(action, level, wait):
        slot = level * width + corner
        if wait:
            arrive(slot)
        action(copy("twin", slot))

    def around(distance, do):
        if distance == 0:
            do(z, True)
            return

        @pl.when(z >= distance)
        def _():
            do(z - distance, True)

        @pl.when(z + distance < depth)
        def _():
            do(z + distance, False)

    def start(descriptor):
        descriptor.start()

    def finish(descriptor):
        descriptor.wait_send()

    own = pltpu.make_async_copy(piece, gathered.at[z * width + me], local_sem)
    own.start()
    column(start, z, 0, True)

    for turn in range(1, depth + 2):
        if turn < depth:
            def onward(level, rising, turn=turn):
                arrive(level * width + me)
                column(start, level, turn, rising)
            around(turn, onward)
        if turn - 1 < depth:
            around(turn - 1, lambda level, rising: plane(start, level, True))
        if turn >= 2:
            around(turn - 2, lambda level, rising: far(start, level, True))
    for distance in range(depth):
        def rest(level, rising, distance=distance):
            for other in (twin, flat + twin - me, upright + twin - me, corner + twin - me):
                arrive(level * width + other)
            column(finish, level, distance, rising)
            plane(finish, level, False)
            far(finish, level, False)
        around(distance, rest)
    own.wait()


def gather_all(piece):
    depth, width = lax.axis_size("st"), lax.axis_size("mem")
    if width != 8 or depth < 2:
        return lax.all_gather(piece, ("st", "mem"))
    return pl.pallas_call(
        gather_kernel,
        out_shape=jax.ShapeDtypeStruct((depth * width, *piece.shape), piece.dtype),
        in_specs=[pl.BlockSpec(memory_space=pl.ANY)],
        out_specs=pl.BlockSpec(memory_space=pltpu.VMEM),
        scratch_shapes=[
            pltpu.SemaphoreType.DMA((5 * depth * width,)),
            pltpu.SemaphoreType.DMA((depth * width,)),
            pltpu.SemaphoreType.DMA,
        ],
        compiler_params=pltpu.CompilerParams(collective_id=0, has_side_effects=True, vmem_limit_bytes=GATHER_LIMIT),
    )(piece)


def gathered_shards(ensemble, obs_values, obs_sigma, obs_operator, block_cols, batch_order):
    size = obs_operator.shape[-1]
    row_count, width = ensemble.shape
    blocks = row_count // size
    mem_count, st_count = lax.axis_size("mem"), lax.axis_size("st")
    members = width * mem_count
    batches, obs_blocks, _ = block_cols.shape
    gathered = gather_all(ensemble.T)
    place = jnp.stack([lax.axis_index("mem"), lax.axis_index("st")]).astype(jnp.int32)
    smem = pl.BlockSpec(memory_space=pltpu.SMEM)
    vmem = pl.BlockSpec(memory_space=pltpu.VMEM)
    _, analysis, logw, ess = pl.pallas_call(
        functools.partial(kernel, members),
        out_shape=(
            jax.ShapeDtypeStruct(gathered.shape, jnp.float32),
            jax.ShapeDtypeStruct((width, row_count), jnp.float32),
            jax.ShapeDtypeStruct((1, width), jnp.float32),
            jax.ShapeDtypeStruct((1, 1), jnp.float32),
        ),
        in_specs=[smem, smem, smem, vmem, vmem, vmem, vmem],
        out_specs=(vmem, vmem, vmem, vmem),
        input_output_aliases={6: 0},
        scratch_shapes=[
            pltpu.VMEM((obs_blocks, 2, members, 2 * size), jnp.bfloat16),
            pltpu.VMEM((obs_blocks, 3 * size, members), jnp.bfloat16),
            pltpu.VMEM((size * obs_blocks, size), jnp.float32),
            pltpu.VMEM((3, size, PANEL * obs_blocks), jnp.float32),
            pltpu.VMEM((8, members), jnp.float32),
            pltpu.VMEM((obs_blocks, 2 * size, members), jnp.bfloat16),
            pltpu.VMEM((obs_blocks, size, members), jnp.float32),
            pltpu.VMEM((obs_blocks, 2 * size, 2 * size), jnp.bfloat16),
        ],
        compiler_params=pltpu.CompilerParams(vmem_limit_bytes=32 << 20),
    )(batch_order, block_cols.transpose(0, 2, 1), place, obs_values, obs_sigma, obs_operator, gathered)
    return analysis.T, logw.reshape(width), ess.reshape(())


def solve_blocks(moment, target):
    factor = jnp.linalg.cholesky(moment)
    return jax.vmap(lambda lower, right: jax.scipy.linalg.cho_solve((lower, True), right))(
        factor, target
    )


def reduced_shards(ensemble, obs_values, obs_sigma, obs_operator, block_cols, batch_order):
    block_size = obs_operator.shape[-1]
    row_count, mem_dev = ensemble.shape
    nblocks = row_count // block_size
    members = mem_dev * lax.axis_size("mem")
    batches, obs_blocks, col_count = block_cols.shape
    temper = 1.0 / math.sqrt(batches * obs_blocks * block_size)
    offset = lax.axis_index("st") * nblocks
    states = ensemble.reshape(nblocks, block_size, mem_dev)
    eye = jnp.eye(block_size, dtype=jnp.float32)
    slots = jnp.arange(nblocks, dtype=jnp.int32)
    loglik = jnp.zeros((mem_dev,), jnp.float32)
    for batch_step in range(batches):
        chosen = batch_order[batch_step]
        operator_now = lax.dynamic_index_in_dim(obs_operator, chosen, 0, keepdims=False)
        columns = lax.dynamic_index_in_dim(block_cols, chosen, 0, keepdims=False)
        values_now = lax.dynamic_index_in_dim(obs_values, chosen, 0, keepdims=False)
        sigma_now = lax.dynamic_index_in_dim(obs_sigma, chosen, 0, keepdims=False)
        local_ids = columns.reshape(-1) - offset
        selector = (local_ids[:, None] == slots[None, :]).astype(jnp.float32)
        picked = jnp.einsum("ps,sim->pim", selector, states, precision=precise)
        picked = picked.reshape(obs_blocks, col_count, block_size, mem_dev)
        partial_value = jnp.einsum("bkij,bkjm->bim", operator_now, picked, precision=precise)
        image = lax.psum(partial_value, "st")
        misfit = (values_now[:, :, None] - image) / sigma_now[:, :, None]
        loglik = loglik - 0.5 * temper * jnp.sum(misfit * misfit, axis=(0, 1))
        center = lax.psum(jnp.sum(image, axis=2), "mem") / members
        anomaly = image - center[:, :, None]
        moment_sum, cross_sum = lax.psum(
            (
                jnp.einsum("bim,bjm->bij", anomaly, anomaly, precision=precise),
                jnp.einsum("bkim,bjm->bkij", picked, anomaly, precision=precise),
            ),
            "mem",
        )
        moment = moment_sum / (members - 1) + eye * (sigma_now * sigma_now)[:, :, None]
        cross = cross_sum / (members - 1)
        target = (values_now - center)[:, :, None] - 0.5 * anomaly
        weights = solve_blocks(moment, target)
        change = jnp.einsum("bkij,bjm->bkim", cross, weights, precision=precise)
        change = change.reshape(obs_blocks * col_count, block_size, mem_dev)
        states = states + jnp.einsum("ps,pim->sim", selector, change, precision=precise)
    largest_local = jnp.max(loglik)
    largest = lax.pmax(largest_local, "mem")
    scaled = jnp.exp(loglik - largest)
    summed, squares = lax.psum((jnp.sum(scaled), jnp.sum(scaled * scaled)), "mem")
    log_weights = loglik - largest - jnp.log(summed)
    ess = summed * summed / squares
    return (states.reshape(row_count, mem_dev), log_weights, ess)


def shards(ensemble, *others):
    devices = lax.axis_size("mem") * lax.axis_size("st")
    fits = 4 * ensemble.size * devices <= GATHER_LIMIT
    return (gathered_shards if fits else reduced_shards)(ensemble, *others)


def solution(mesh):
    placed = (P("st", "mem"), P(), P(), P(), P(), P())
    return jax.shard_map(
        shards,
        mesh=mesh,
        in_specs=placed,
        out_specs=(P("st", "mem"), P("mem"), P()),
        check_vma=False,
    )
```

```python
import functools
import math

import jax
import jax.numpy as jnp
from jax import lax
from jax.experimental import pallas as pl
from jax.experimental.pallas import tpu as pltpu
from jax.sharding import PartitionSpec as P

precise = lax.Precision.HIGHEST
PANEL = 16
SUB = 8
GATHER_LIMIT = 16 << 20
CUTS = 2
REACH = 1


def halves(x):
    high = x.astype(jnp.bfloat16)
    return high, (x - high.astype(jnp.float32)).astype(jnp.bfloat16)


def thirds(x):
    high = x.astype(jnp.bfloat16)
    rest = x - high.astype(jnp.float32)
    mid = rest.astype(jnp.bfloat16)
    return high, mid, (rest - mid.astype(jnp.float32)).astype(jnp.bfloat16)


def mul_nn(a, b):
    return lax.dot_general(a, b, (((1,), (0,)), ((), ())), preferred_element_type=jnp.float32)


def mul_nt(a, b):
    return lax.dot_general(a, b, (((1,), (1,)), ((), ())), preferred_element_type=jnp.float32)


def factor(moments, crossed, obs_blocks, size):
    lanes = lax.broadcasted_iota(jnp.int32, (obs_blocks, size), 1)
    own = lanes % obs_blocks == lax.broadcasted_iota(jnp.int32, (obs_blocks, size), 0)
    own = own.astype(jnp.float32)[:, : PANEL * obs_blocks]

    def spread(rows, lane):
        count = len(rows)
        tall = jnp.concatenate(rows, axis=0)
        tall = jnp.broadcast_to(tall[:, lane : lane + 1], (count * obs_blocks, size))
        return [tall[r * obs_blocks : (r + 1) * obs_blocks] for r in range(count)]

    def line(r):
        return slice(r * obs_blocks, (r + 1) * obs_blocks)

    def updates(rhs, low, high):
        parts = []
        for k in range(3):
            wide = [jnp.broadcast_to(crossed[k, r : r + 1, :], own.shape) * own for r in range(low, high)]
            parts.append(jnp.concatenate(wide, axis=0).astype(jnp.bfloat16))
        main = mul_nn(jnp.concatenate([parts[0], parts[1]], axis=1), rhs[0])
        return main[:, size:] + mul_nn(jnp.concatenate([parts[2], parts[0]], axis=1), rhs[1]) + main[:, :size]

    rows = [moments[line(i), :] for i in range(PANEL)]
    for first in range(0, size, PANEL):
        for sub in range(0, PANEL, SUB):
            base = first + sub
            inside = (lanes >= base) & (lanes < base + SUB)
            entry = {}
            for j in range(SUB):
                for i, value in zip(range(j, SUB), spread(rows[sub + j : sub + SUB], base + j)):
                    entry[i, j] = value
            for i in range(SUB):
                rows[sub + i] = jnp.where(inside, (lanes == base + i).astype(jnp.float32), rows[sub + i])
            for p in range(SUB):
                root = lax.rsqrt(entry[p, p])
                rows[sub + p] = rows[sub + p] * root
                column = {i: entry[i, p] * root for i in range(p + 1, SUB)}
                for i in range(p + 1, SUB):
                    for j in range(p + 1, i + 1):
                        entry[i, j] = entry[i, j] - column[i] * column[j]
                for i in range(p + 1, SUB):
                    rows[sub + i] = rows[sub + i] - column[i] * rows[sub + p]
            for i in range(sub + SUB, PANEL):
                row = jnp.where(inside, 0.0, rows[i])
                for p, value in zip(range(sub, sub + SUB), spread(rows[sub : sub + SUB], first + i)):
                    row = row - value * rows[p]
                rows[i] = row
        for i in range(PANEL - SUB):
            later = first + i // SUB * SUB + SUB
            rows[i] = jnp.where((lanes >= later) & (lanes < first + PANEL), 0.0, rows[i])
        for i in range(PANEL):
            moments[line(first + i), :] = rows[i]
        below = first + PANEL
        if below == size:
            return
        stack = jnp.concatenate(rows, axis=0)
        high, mid, low = thirds(stack)
        across = thirds(stack.T)
        for k in range(3):
            crossed[k, :, :] = across[k].astype(jnp.float32)
        rhs = [
            jnp.concatenate([jnp.concatenate([high, mid], axis=1)] * 2, axis=0),
            jnp.concatenate([high, low], axis=0),
        ]
        inside = (lanes >= first) & (lanes < below)
        change = updates(rhs, below, below + PANEL)
        rows = [jnp.where(inside, 0.0, moments[line(below + i), :]) - change[line(i)] for i in range(PANEL)]
        if below + PANEL < size:
            change = updates(rhs, below + PANEL, size)
            for i in range(size - below - PANEL):
                here = line(below + PANEL + i)
                moments[here, :] = jnp.where(inside, 0.0, moments[here, :]) - change[line(i)]


def kernel(
    members, order, columns, place, values, sigma, operator, gathered,
    states, analysis, logw, ess,
    picks, parts, moments, crossed, misfits, whites, targets, crosses,
):
    batches, obs_blocks, size = values.shape
    _, width, row_count = states.shape
    mem_count = members // width
    blocks = row_count // size
    misfits[...] = jnp.zeros_like(misfits)
    line = lax.broadcasted_iota(jnp.int32, (size, size), 0)
    cols = lax.broadcasted_iota(jnp.int32, (size, size), 1)
    eye = (line == cols).astype(jnp.float32)
    below_diagonal = line >= cols

    def spot(block):
        level = pl.ds((block // blocks) * mem_count, mem_count)
        return level, slice(None), pl.ds(pl.multiple_of((block % blocks) * size, size), size)

    @pl.loop(0, batches)
    def _(step):
        chosen = order[step]
        values_now, sigma_now = values[chosen], sigma[chosen]
        values_t, sigma_t = values_now.T, sigma_now.T
        centers = []
        for b in range(obs_blocks):
            sides = []
            for k in range(2):
                sides.append(states[spot(columns[chosen, k, b])].reshape(members, size))
            high, mid = halves(jnp.concatenate(sides, axis=1))
            picks[b, 0] = high
            picks[b, 1] = mid
            h_high, h_mid = halves(jnp.concatenate([operator[chosen, b, 0], operator[chosen, b, 1]], axis=1))
            image = mul_nt(jnp.concatenate([h_high, h_mid], axis=0), high)
            image = image[:size] + image[size:] + mul_nt(h_high, mid)
            value, deviation = values_t[:, b : b + 1], sigma_t[:, b : b + 1]
            misfit = (value - image) * (1.0 / deviation)
            misfits[...] += jnp.sum((misfit * misfit).reshape(size // 8, 8, members), axis=0)
            center = jnp.sum(image, axis=1, keepdims=True) * (1.0 / members)
            centers.append(center)
            high, mid, low = thirds(image - center)
            tall = jnp.concatenate([high, mid, low], axis=0)
            parts[b] = tall
        for b in range(obs_blocks):
            tall = parts[b]
            high, low = tall[:size], tall[2 * size :]
            deviation = sigma_t[:, b : b + 1]
            product = mul_nt(tall, tall[: 2 * size])
            total = (product[size : 2 * size, size:] + product[2 * size :, :size]) + mul_nt(high, low)
            total = (product[:size, size:] + product[size : 2 * size, :size] + total) + product[:size, :size]
            moments[pl.ds(b, size, stride=obs_blocks), :] = total * (1.0 / (members - 1)) + eye * (deviation * deviation)
        offsets = values_now - jnp.concatenate(centers, axis=1).T

        factor(moments, crossed, obs_blocks, size)

        for b in range(obs_blocks):
            lower = jnp.where(below_diagonal, moments[pl.ds(b, size, stride=obs_blocks), :], 0.0)
            shift = jnp.sum(lower * offsets[b : b + 1, :], axis=1, keepdims=True)
            l_high, l_mid, l_low = thirds(lower)
            tall = parts[b]
            pair = jnp.concatenate([jnp.concatenate([l_high, l_high], axis=1), jnp.concatenate([l_mid, l_mid], axis=1)], axis=0)
            first = mul_nn(pair, tall[: 2 * size])
            last = mul_nn(jnp.concatenate([l_low, l_high], axis=1), jnp.concatenate([tall[:size], tall[2 * size :]], axis=0))
            whitened = first[:size] + (first[size:] + last)
            whites[b] = jnp.concatenate(halves(whitened), axis=0)
            targets[b] = (shift - 0.5 * whitened) * (1.0 / (members - 1))
        for b in range(obs_blocks):
            cross = mul_nn(whites[b], picks[b, 0])
            cross = cross[:size] + cross[size:] + mul_nn(whites[b, :size], picks[b, 1])
            crosses[b] = jnp.concatenate(halves(cross), axis=0)
        for b in range(obs_blocks):
            t_high, t_mid = halves(targets[b].T)
            change = mul_nn(jnp.concatenate([t_high, t_high], axis=1), crosses[b])
            change = change + mul_nn(t_mid, crosses[b, :size])
            for k in range(2):
                where = spot(columns[chosen, k, b])
                states[where] += change[:, k * size : (k + 1) * size].reshape(mem_count, width, size)

    temper = 1.0 / math.sqrt(batches * obs_blocks * size)
    likely = -0.5 * temper * jnp.sum(misfits[...], axis=0, keepdims=True)
    largest = jnp.max(likely, axis=1, keepdims=True)
    scaled = jnp.exp(likely - largest)
    summed = jnp.sum(scaled, axis=1, keepdims=True)
    squares = jnp.sum(scaled * scaled, axis=1, keepdims=True)
    ess[...] = summed * summed / squares
    logs = jnp.broadcast_to(likely - largest - jnp.log(summed), (8, members))
    logs = pltpu.roll(logs, lax.rem(members - place[0] * width, members), 1)
    logw[...] = logs[:1, :width]
    analysis[...] = states[place[1] * mem_count + place[0]]


MESH = pl.DeviceIdType.MESH


def gather_kernel(piece, gathered, send_sems, recv_sems, local_sem):
    me, z = lax.axis_index("mem"), lax.axis_index("st")
    depth, width = lax.axis_size("st"), lax.axis_size("mem")
    core, bit = me % 2, (me // 2) % 2
    twin = me + 1 - 2 * core
    flat = me + 2 - 4 * bit
    upright = (me + width // 2) % width
    corner = (flat + width // 2) % width
    kinds = {"up": 0, "down": 1, "flat": 2, "upright": 3, "twin": 4}
    targets = {"up": (me, z + 1), "down": (me, z - 1), "flat": (flat, z), "upright": (upright, z), "twin": (twin, z)}
    share = piece.shape[0] // CUTS

    def copy(kind, slot, cut, source=None):
        rows = pl.ds(cut * share, share)
        here = gathered.at[slot, rows]
        return pltpu.make_async_remote_copy(
            src_ref=here if source is None else source.at[rows],
            dst_ref=here,
            send_sem=send_sems.at[(kinds[kind] * depth * width + slot) * CUTS + cut],
            recv_sem=recv_sems.at[slot * CUTS + cut],
            device_id=targets[kind],
            device_id_type=MESH,
        )

    def arrive(slot, cut):
        copy("twin", slot, cut).wait_recv()

    barrier = pltpu.get_barrier_semaphore()
    for kind in ("flat", "upright", "twin"):
        pl.semaphore_signal(barrier, inc=1, device_id=targets[kind], device_id_type=MESH)

    @pl.when(z < depth - 1)
    def _():
        pl.semaphore_signal(barrier, inc=1, device_id=targets["up"], device_id_type=MESH)

    @pl.when(z > 0)
    def _():
        pl.semaphore_signal(barrier, inc=1, device_id=targets["down"], device_id_type=MESH)

    @pl.when((z > 0) & (z < depth - 1))
    def _():
        pl.semaphore_wait(barrier, 5)

    @pl.when((z == 0) | (z == depth - 1))
    def _():
        pl.semaphore_wait(barrier, 4)

    def along(action, slot, cut, distance, rising, source=None):
        if distance == 0 or rising:
            @pl.when(z < depth - 1)
            def _():
                action(copy("up", slot, cut, source))

        if distance == 0 or not rising:
            @pl.when(z > 0)
            def _():
                action(copy("down", slot, cut, source))

    def column(action, level, cut, distance, rising, wait):
        slot = level * width + me
        source = piece if distance == 0 else None
        if wait:
            arrive(slot, cut)
        along(action, slot, cut, distance, rising, source)
        for kind in ("flat", "upright", "twin"):
            action(copy(kind, slot, cut, source))

    def plane(action, level, cut, distance, rising, wait):
        for first, onward, parity in ((flat, "upright", 1), (upright, "flat", 0)):
            slot = level * width + first
            if wait:
                arrive(slot, cut)
            if distance == 0 or distance > REACH:
                @pl.when((level + cut) % 2 == parity)
                def _():
                    action(copy(onward, slot, cut))

            action(copy("twin", slot, cut))

    def far(action, level, cut, distance, rising, wait):
        slot = level * width + corner
        if wait:
            arrive(slot, cut)
        if distance < REACH:
            along(action, slot, cut, distance, rising)
        action(copy("twin", slot, cut))

    def around(distance, do):
        if distance == 0:
            do(z, True)
            return

        @pl.when(z >= distance)
        def _():
            do(z - distance, True)

        @pl.when(z + distance < depth)
        def _():
            do(z + distance, False)

    def start(descriptor):
        descriptor.start()

    def finish(descriptor):
        descriptor.wait_send()

    own = pltpu.make_async_copy(piece, gathered.at[z * width + me], local_sem)
    own.start()

    for turn in range(0, depth + 2):
        for part, late in ((column, 0), (plane, 1), (far, 2)):
            distance = turn - late
            if 0 <= distance < depth:
                def go(level, rising, part=part, distance=distance):
                    for cut in range(CUTS):
                        part(start, level, cut, distance, rising, not (part is column and distance == 0))
                around(distance, go)
    for distance in range(depth):
        def rest(level, rising, distance=distance):
            for cut in range(CUTS):
                for other in (twin, flat + twin - me, upright + twin - me, corner + twin - me):
                    arrive(level * width + other, cut)
                for part in (column, plane, far):
                    part(finish, level, cut, distance, rising, False)
        around(distance, rest)
    own.wait()


def gather_all(piece):
    depth, width = lax.axis_size("st"), lax.axis_size("mem")
    if width != 8 or depth < 2:
        return lax.all_gather(piece, ("st", "mem"))
    return pl.pallas_call(
        gather_kernel,
        out_shape=jax.ShapeDtypeStruct((depth * width, *piece.shape), piece.dtype),
        in_specs=[pl.BlockSpec(memory_space=pl.ANY)],
        out_specs=pl.BlockSpec(memory_space=pltpu.VMEM),
        scratch_shapes=[
            pltpu.SemaphoreType.DMA((5 * depth * width * CUTS,)),
            pltpu.SemaphoreType.DMA((depth * width * CUTS,)),
            pltpu.SemaphoreType.DMA,
        ],
        compiler_params=pltpu.CompilerParams(collective_id=0, has_side_effects=True, vmem_limit_bytes=GATHER_LIMIT),
    )(piece)


def gathered_shards(ensemble, obs_values, obs_sigma, obs_operator, block_cols, batch_order):
    size = obs_operator.shape[-1]
    row_count, width = ensemble.shape
    blocks = row_count // size
    mem_count, st_count = lax.axis_size("mem"), lax.axis_size("st")
    members = width * mem_count
    batches, obs_blocks, _ = block_cols.shape
    gathered = gather_all(ensemble.T)
    place = jnp.stack([lax.axis_index("mem"), lax.axis_index("st")]).astype(jnp.int32)
    smem = pl.BlockSpec(memory_space=pltpu.SMEM)
    vmem = pl.BlockSpec(memory_space=pltpu.VMEM)
    _, analysis, logw, ess = pl.pallas_call(
        functools.partial(kernel, members),
        out_shape=(
            jax.ShapeDtypeStruct(gathered.shape, jnp.float32),
            jax.ShapeDtypeStruct((width, row_count), jnp.float32),
            jax.ShapeDtypeStruct((1, width), jnp.float32),
            jax.ShapeDtypeStruct((1, 1), jnp.float32),
        ),
        in_specs=[smem, smem, smem, vmem, vmem, vmem, vmem],
        out_specs=(vmem, vmem, vmem, vmem),
        input_output_aliases={6: 0},
        scratch_shapes=[
            pltpu.VMEM((obs_blocks, 2, members, 2 * size), jnp.bfloat16),
            pltpu.VMEM((obs_blocks, 3 * size, members), jnp.bfloat16),
            pltpu.VMEM((size * obs_blocks, size), jnp.float32),
            pltpu.VMEM((3, size, PANEL * obs_blocks), jnp.float32),
            pltpu.VMEM((8, members), jnp.float32),
            pltpu.VMEM((obs_blocks, 2 * size, members), jnp.bfloat16),
            pltpu.VMEM((obs_blocks, size, members), jnp.float32),
            pltpu.VMEM((obs_blocks, 2 * size, 2 * size), jnp.bfloat16),
        ],
        compiler_params=pltpu.CompilerParams(vmem_limit_bytes=32 << 20),
    )(batch_order, block_cols.transpose(0, 2, 1), place, obs_values, obs_sigma, obs_operator, gathered)
    return analysis.T, logw.reshape(width), ess.reshape(())


def solve_blocks(moment, target):
    factor = jnp.linalg.cholesky(moment)
    return jax.vmap(lambda lower, right: jax.scipy.linalg.cho_solve((lower, True), right))(
        factor, target
    )


def reduced_shards(ensemble, obs_values, obs_sigma, obs_operator, block_cols, batch_order):
    block_size = obs_operator.shape[-1]
    row_count, mem_dev = ensemble.shape
    nblocks = row_count // block_size
    members = mem_dev * lax.axis_size("mem")
    batches, obs_blocks, col_count = block_cols.shape
    temper = 1.0 / math.sqrt(batches * obs_blocks * block_size)
    offset = lax.axis_index("st") * nblocks
    states = ensemble.reshape(nblocks, block_size, mem_dev)
    eye = jnp.eye(block_size, dtype=jnp.float32)
    slots = jnp.arange(nblocks, dtype=jnp.int32)
    loglik = jnp.zeros((mem_dev,), jnp.float32)
    for batch_step in range(batches):
        chosen = batch_order[batch_step]
        operator_now = lax.dynamic_index_in_dim(obs_operator, chosen, 0, keepdims=False)
        columns = lax.dynamic_index_in_dim(block_cols, chosen, 0, keepdims=False)
        values_now = lax.dynamic_index_in_dim(obs_values, chosen, 0, keepdims=False)
        sigma_now = lax.dynamic_index_in_dim(obs_sigma, chosen, 0, keepdims=False)
        local_ids = columns.reshape(-1) - offset
        selector = (local_ids[:, None] == slots[None, :]).astype(jnp.float32)
        picked = jnp.einsum("ps,sim->pim", selector, states, precision=precise)
        picked = picked.reshape(obs_blocks, col_count, block_size, mem_dev)
        partial_value = jnp.einsum("bkij,bkjm->bim", operator_now, picked, precision=precise)
        image = lax.psum(partial_value, "st")
        misfit = (values_now[:, :, None] - image) / sigma_now[:, :, None]
        loglik = loglik - 0.5 * temper * jnp.sum(misfit * misfit, axis=(0, 1))
        center = lax.psum(jnp.sum(image, axis=2), "mem") / members
        anomaly = image - center[:, :, None]
        moment_sum, cross_sum = lax.psum(
            (
                jnp.einsum("bim,bjm->bij", anomaly, anomaly, precision=precise),
                jnp.einsum("bkim,bjm->bkij", picked, anomaly, precision=precise),
            ),
            "mem",
        )
        moment = moment_sum / (members - 1) + eye * (sigma_now * sigma_now)[:, :, None]
        cross = cross_sum / (members - 1)
        target = (values_now - center)[:, :, None] - 0.5 * anomaly
        weights = solve_blocks(moment, target)
        change = jnp.einsum("bkij,bjm->bkim", cross, weights, precision=precise)
        change = change.reshape(obs_blocks * col_count, block_size, mem_dev)
        states = states + jnp.einsum("ps,pim->sim", selector, change, precision=precise)
    largest_local = jnp.max(loglik)
    largest = lax.pmax(largest_local, "mem")
    scaled = jnp.exp(loglik - largest)
    summed, squares = lax.psum((jnp.sum(scaled), jnp.sum(scaled * scaled)), "mem")
    log_weights = loglik - largest - jnp.log(summed)
    ess = summed * summed / squares
    return (states.reshape(row_count, mem_dev), log_weights, ess)


def shards(ensemble, *others):
    devices = lax.axis_size("mem") * lax.axis_size("st")
    fits = 4 * ensemble.size * devices <= GATHER_LIMIT
    return (gathered_shards if fits else reduced_shards)(ensemble, *others)


def solution(mesh):
    placed = (P("st", "mem"), P(), P(), P(), P(), P())
    return jax.shard_map(
        shards,
        mesh=mesh,
        in_specs=placed,
        out_specs=(P("st", "mem"), P("mem"), P()),
        check_vma=False,
    )
```

```python
import functools
import math

import jax
import jax.numpy as jnp
from jax import lax
from jax.experimental import pallas as pl
from jax.experimental.pallas import tpu as pltpu
from jax.sharding import PartitionSpec as P

precise = lax.Precision.HIGHEST
PANEL = 16
SUB = 8
GATHER_LIMIT = 16 << 20
CUTS = 2
REACH = 1


def halves(x):
    high = x.astype(jnp.bfloat16)
    return high, (x - high.astype(jnp.float32)).astype(jnp.bfloat16)


def thirds(x):
    high = x.astype(jnp.bfloat16)
    rest = x - high.astype(jnp.float32)
    mid = rest.astype(jnp.bfloat16)
    return high, mid, (rest - mid.astype(jnp.float32)).astype(jnp.bfloat16)


def mul_nn(a, b):
    return lax.dot_general(a, b, (((1,), (0,)), ((), ())), preferred_element_type=jnp.float32)


def mul_nt(a, b):
    return lax.dot_general(a, b, (((1,), (1,)), ((), ())), preferred_element_type=jnp.float32)


def factor(moments, crossed, obs_blocks, size):
    lanes = lax.broadcasted_iota(jnp.int32, (obs_blocks, size), 1)
    own = lanes % obs_blocks == lax.broadcasted_iota(jnp.int32, (obs_blocks, size), 0)
    own = own.astype(jnp.float32)[:, : PANEL * obs_blocks]

    def spread(rows, lane):
        count = len(rows)
        tall = jnp.concatenate(rows, axis=0)
        tall = jnp.broadcast_to(tall[:, lane : lane + 1], (count * obs_blocks, size))
        return [tall[r * obs_blocks : (r + 1) * obs_blocks] for r in range(count)]

    def line(r):
        return slice(r * obs_blocks, (r + 1) * obs_blocks)

    def updates(rhs, low, high):
        parts = []
        for k in range(3):
            wide = [jnp.broadcast_to(crossed[k, r : r + 1, :], own.shape) * own for r in range(low, high)]
            parts.append(jnp.concatenate(wide, axis=0).astype(jnp.bfloat16))
        main = mul_nn(jnp.concatenate([parts[0], parts[1]], axis=1), rhs[0])
        return main[:, size:] + mul_nn(jnp.concatenate([parts[2], parts[0]], axis=1), rhs[1]) + main[:, :size]

    rows = [moments[line(i), :] for i in range(PANEL)]
    pending = []
    for first in range(0, size, PANEL):
        for sub in range(0, PANEL, SUB):
            base = first + sub
            inside = (lanes >= base) & (lanes < base + SUB)
            entry = {}
            for j in range(SUB):
                for i, value in zip(range(j, SUB), spread(rows[sub + j : sub + SUB], base + j)):
                    entry[i, j] = value
            while pending:
                pending.pop()()
            for i in range(SUB):
                rows[sub + i] = jnp.where(inside, (lanes == base + i).astype(jnp.float32), rows[sub + i])
            for p in range(SUB):
                root = lax.rsqrt(entry[p, p])
                rows[sub + p] = rows[sub + p] * root
                column = {i: entry[i, p] * root for i in range(p + 1, SUB)}
                for i in range(p + 1, SUB):
                    for j in range(p + 1, i + 1):
                        entry[i, j] = entry[i, j] - column[i] * column[j]
                for i in range(p + 1, SUB):
                    rows[sub + i] = rows[sub + i] - column[i] * rows[sub + p]
            for i in range(sub + SUB, PANEL):
                row = jnp.where(inside, 0.0, rows[i])
                for p, value in zip(range(sub, sub + SUB), spread(rows[sub : sub + SUB], first + i)):
                    row = row - value * rows[p]
                rows[i] = row
        for i in range(PANEL - SUB):
            later = first + i // SUB * SUB + SUB
            rows[i] = jnp.where((lanes >= later) & (lanes < first + PANEL), 0.0, rows[i])
        for i in range(PANEL):
            moments[line(first + i), :] = rows[i]
        below = first + PANEL
        if below == size:
            return
        stack = jnp.concatenate(rows, axis=0)
        high, mid, low = thirds(stack)
        across = thirds(stack.T)
        for k in range(3):
            crossed[k, :, :] = across[k].astype(jnp.float32)
        rhs = [
            jnp.concatenate([jnp.concatenate([high, mid], axis=1)] * 2, axis=0),
            jnp.concatenate([high, low], axis=0),
        ]
        inside = (lanes >= first) & (lanes < below)
        change = updates(rhs, below, below + PANEL)
        rows = [jnp.where(inside, 0.0, moments[line(below + i), :]) - change[line(i)] for i in range(PANEL)]
        if below + PANEL < size:
            def later(rhs=rhs, inside=inside, low=below + PANEL):
                change = updates(rhs, low, size)
                for i in range(size - low):
                    here = line(low + i)
                    moments[here, :] = jnp.where(inside, 0.0, moments[here, :]) - change[line(i)]
            pending.append(later)


def kernel(
    members, order, columns, place, values, sigma, operator, gathered,
    states, analysis, logw, ess,
    picks, parts, moments, crossed, misfits, whites, targets, crosses,
):
    batches, obs_blocks, size = values.shape
    _, width, row_count = states.shape
    mem_count = members // width
    blocks = row_count // size
    misfits[...] = jnp.zeros_like(misfits)
    line = lax.broadcasted_iota(jnp.int32, (size, size), 0)
    cols = lax.broadcasted_iota(jnp.int32, (size, size), 1)
    eye = (line == cols).astype(jnp.float32)
    below_diagonal = line >= cols

    def spot(block):
        level = pl.ds((block // blocks) * mem_count, mem_count)
        return level, slice(None), pl.ds(pl.multiple_of((block % blocks) * size, size), size)

    @pl.loop(0, batches)
    def _(step):
        chosen = order[step]
        values_now, sigma_now = values[chosen], sigma[chosen]
        values_t, sigma_t = values_now.T, sigma_now.T
        centers = []
        for b in range(obs_blocks):
            sides = []
            for k in range(2):
                sides.append(states[spot(columns[chosen, k, b])].reshape(members, size))
            high, mid = halves(jnp.concatenate(sides, axis=1))
            picks[b, 0] = high
            picks[b, 1] = mid
            h_high, h_mid = halves(jnp.concatenate([operator[chosen, b, 0], operator[chosen, b, 1]], axis=1))
            image = mul_nt(jnp.concatenate([h_high, h_mid], axis=0), high)
            image = image[:size] + image[size:] + mul_nt(h_high, mid)
            value, deviation = values_t[:, b : b + 1], sigma_t[:, b : b + 1]
            misfit = (value - image) * (1.0 / deviation)
            misfits[...] += jnp.sum((misfit * misfit).reshape(size // 8, 8, members), axis=0)
            center = jnp.sum(image, axis=1, keepdims=True) * (1.0 / members)
            centers.append(center)
            high, mid, low = thirds(image - center)
            tall = jnp.concatenate([high, mid, low], axis=0)
            parts[b] = tall
        for b in range(obs_blocks):
            tall = parts[b]
            deviation = sigma_t[:, b : b + 1]
            product = mul_nt(tall, tall[: 2 * size])
            cross = product[:size, size:] + product[2 * size :, :size]
            total = (product[size : 2 * size, size:] + (cross + cross.T)) + product[:size, :size]
            moments[pl.ds(b, size, stride=obs_blocks), :] = total * (1.0 / (members - 1)) + eye * (deviation * deviation)
        offsets = values_now - jnp.concatenate(centers, axis=1).T

        factor(moments, crossed, obs_blocks, size)

        for b in range(obs_blocks):
            lower = jnp.where(below_diagonal, moments[pl.ds(b, size, stride=obs_blocks), :], 0.0)
            shift = jnp.sum(lower * offsets[b : b + 1, :], axis=1, keepdims=True)
            l_high, l_mid, l_low = thirds(lower)
            tall = parts[b]
            pair = jnp.concatenate([jnp.concatenate([l_high, l_high], axis=1), jnp.concatenate([l_mid, l_mid], axis=1)], axis=0)
            first = mul_nn(pair, tall[: 2 * size])
            last = mul_nn(jnp.concatenate([l_low, l_high], axis=1), jnp.concatenate([tall[:size], tall[2 * size :]], axis=0))
            whitened = first[:size] + (first[size:] + last)
            whites[b] = jnp.concatenate(halves(whitened), axis=0)
            targets[b] = (shift - 0.5 * whitened) * (1.0 / (members - 1))
        for b in range(obs_blocks):
            cross = mul_nn(whites[b], picks[b, 0])
            cross = cross[:size] + cross[size:] + mul_nn(whites[b, :size], picks[b, 1])
            crosses[b] = jnp.concatenate(halves(cross), axis=0)
        for b in range(obs_blocks):
            t_high, t_mid = halves(targets[b].T)
            change = mul_nn(jnp.concatenate([t_high, t_high], axis=1), crosses[b])
            change = change + mul_nn(t_mid, crosses[b, :size])
            for k in range(2):
                where = spot(columns[chosen, k, b])
                states[where] += change[:, k * size : (k + 1) * size].reshape(mem_count, width, size)

    temper = 1.0 / math.sqrt(batches * obs_blocks * size)
    likely = -0.5 * temper * jnp.sum(misfits[...], axis=0, keepdims=True)
    largest = jnp.max(likely, axis=1, keepdims=True)
    scaled = jnp.exp(likely - largest)
    summed = jnp.sum(scaled, axis=1, keepdims=True)
    squares = jnp.sum(scaled * scaled, axis=1, keepdims=True)
    ess[...] = summed * summed / squares
    logs = jnp.broadcast_to(likely - largest - jnp.log(summed), (8, members))
    logs = pltpu.roll(logs, lax.rem(members - place[0] * width, members), 1)
    logw[...] = logs[:1, :width]
    analysis[...] = states[place[1] * mem_count + place[0]]


MESH = pl.DeviceIdType.MESH


def gather_kernel(piece, gathered, send_sems, recv_sems, local_sem):
    me, z = lax.axis_index("mem"), lax.axis_index("st")
    depth, width = lax.axis_size("st"), lax.axis_size("mem")
    core, bit = me % 2, (me // 2) % 2
    twin = me + 1 - 2 * core
    flat = me + 2 - 4 * bit
    upright = (me + width // 2) % width
    corner = (flat + width // 2) % width
    kinds = {"up": 0, "down": 1, "flat": 2, "upright": 3, "twin": 4}
    targets = {"up": (me, z + 1), "down": (me, z - 1), "flat": (flat, z), "upright": (upright, z), "twin": (twin, z)}
    share = piece.shape[0] // CUTS

    def copy(kind, slot, cut, source=None):
        rows = pl.ds(cut * share, share)
        here = gathered.at[slot, rows]
        return pltpu.make_async_remote_copy(
            src_ref=here if source is None else source.at[rows],
            dst_ref=here,
            send_sem=send_sems.at[(kinds[kind] * depth * width + slot) * CUTS + cut],
            recv_sem=recv_sems.at[slot * CUTS + cut],
            device_id=targets[kind],
            device_id_type=MESH,
        )

    def arrive(slot, cut):
        copy("twin", slot, cut).wait_recv()

    barrier = pltpu.get_barrier_semaphore()
    for kind in ("flat", "upright", "twin"):
        pl.semaphore_signal(barrier, inc=1, device_id=targets[kind], device_id_type=MESH)

    @pl.when(z < depth - 1)
    def _():
        pl.semaphore_signal(barrier, inc=1, device_id=targets["up"], device_id_type=MESH)

    @pl.when(z > 0)
    def _():
        pl.semaphore_signal(barrier, inc=1, device_id=targets["down"], device_id_type=MESH)

    @pl.when((z > 0) & (z < depth - 1))
    def _():
        pl.semaphore_wait(barrier, 5)

    @pl.when((z == 0) | (z == depth - 1))
    def _():
        pl.semaphore_wait(barrier, 4)

    def along(action, slot, cut, distance, rising, source=None):
        if distance == 0 or rising:
            @pl.when(z < depth - 1)
            def _():
                action(copy("up", slot, cut, source))

        if distance == 0 or not rising:
            @pl.when(z > 0)
            def _():
                action(copy("down", slot, cut, source))

    def column(action, level, cut, distance, rising, wait):
        slot = level * width + me
        source = piece if distance == 0 else None
        if wait:
            arrive(slot, cut)
        along(action, slot, cut, distance, rising, source)
        for kind in ("flat", "upright", "twin"):
            action(copy(kind, slot, cut, source))

    def plane(action, level, cut, distance, rising, wait):
        for first, onward, parity in ((flat, "upright", 1), (upright, "flat", 0)):
            slot = level * width + first
            if wait:
                arrive(slot, cut)
            if distance == 0 or distance > REACH:
                @pl.when((level + cut) % 2 == parity)
                def _():
                    action(copy(onward, slot, cut))

            action(copy("twin", slot, cut))

    def far(action, level, cut, distance, rising, wait):
        slot = level * width + corner
        if wait:
            arrive(slot, cut)
        if distance < REACH:
            along(action, slot, cut, distance, rising)
        action(copy("twin", slot, cut))

    def around(distance, do):
        if distance == 0:
            do(z, True)
            return

        @pl.when(z >= distance)
        def _():
            do(z - distance, True)

        @pl.when(z + distance < depth)
        def _():
            do(z + distance, False)

    def start(descriptor):
        descriptor.start()

    def finish(descriptor):
        descriptor.wait_send()

    own = pltpu.make_async_copy(piece, gathered.at[z * width + me], local_sem)
    own.start()

    for turn in range(0, depth + 2):
        for part, late in ((column, 0), (plane, 1), (far, 2)):
            distance = turn - late
            if 0 <= distance < depth:
                def go(level, rising, part=part, distance=distance):
                    for cut in range(CUTS):
                        part(start, level, cut, distance, rising, not (part is column and distance == 0))
                around(distance, go)
    for distance in range(depth):
        def rest(level, rising, distance=distance):
            for cut in range(CUTS):
                for other in (twin, flat + twin - me, upright + twin - me, corner + twin - me):
                    arrive(level * width + other, cut)
                for part in (column, plane, far):
                    part(finish, level, cut, distance, rising, False)
        around(distance, rest)
    own.wait()


def gather_all(piece):
    depth, width = lax.axis_size("st"), lax.axis_size("mem")
    if width != 8 or depth < 2:
        return lax.all_gather(piece, ("st", "mem"))
    return pl.pallas_call(
        gather_kernel,
        out_shape=jax.ShapeDtypeStruct((depth * width, *piece.shape), piece.dtype),
        in_specs=[pl.BlockSpec(memory_space=pl.ANY)],
        out_specs=pl.BlockSpec(memory_space=pltpu.VMEM),
        scratch_shapes=[
            pltpu.SemaphoreType.DMA((5 * depth * width * CUTS,)),
            pltpu.SemaphoreType.DMA((depth * width * CUTS,)),
            pltpu.SemaphoreType.DMA,
        ],
        compiler_params=pltpu.CompilerParams(collective_id=0, has_side_effects=True, vmem_limit_bytes=GATHER_LIMIT),
    )(piece)


def gathered_shards(ensemble, obs_values, obs_sigma, obs_operator, block_cols, batch_order):
    size = obs_operator.shape[-1]
    row_count, width = ensemble.shape
    blocks = row_count // size
    mem_count, st_count = lax.axis_size("mem"), lax.axis_size("st")
    members = width * mem_count
    batches, obs_blocks, _ = block_cols.shape
    gathered = gather_all(ensemble.T)
    place = jnp.stack([lax.axis_index("mem"), lax.axis_index("st")]).astype(jnp.int32)
    smem = pl.BlockSpec(memory_space=pltpu.SMEM)
    vmem = pl.BlockSpec(memory_space=pltpu.VMEM)
    _, analysis, logw, ess = pl.pallas_call(
        functools.partial(kernel, members),
        out_shape=(
            jax.ShapeDtypeStruct(gathered.shape, jnp.float32),
            jax.ShapeDtypeStruct((width, row_count), jnp.float32),
            jax.ShapeDtypeStruct((1, width), jnp.float32),
            jax.ShapeDtypeStruct((1, 1), jnp.float32),
        ),
        in_specs=[smem, smem, smem, vmem, vmem, vmem, vmem],
        out_specs=(vmem, vmem, vmem, vmem),
        input_output_aliases={6: 0},
        scratch_shapes=[
            pltpu.VMEM((obs_blocks, 2, members, 2 * size), jnp.bfloat16),
            pltpu.VMEM((obs_blocks, 3 * size, members), jnp.bfloat16),
            pltpu.VMEM((size * obs_blocks, size), jnp.float32),
            pltpu.VMEM((3, size, PANEL * obs_blocks), jnp.float32),
            pltpu.VMEM((8, members), jnp.float32),
            pltpu.VMEM((obs_blocks, 2 * size, members), jnp.bfloat16),
            pltpu.VMEM((obs_blocks, size, members), jnp.float32),
            pltpu.VMEM((obs_blocks, 2 * size, 2 * size), jnp.bfloat16),
        ],
        compiler_params=pltpu.CompilerParams(vmem_limit_bytes=32 << 20),
    )(batch_order, block_cols.transpose(0, 2, 1), place, obs_values, obs_sigma, obs_operator, gathered)
    return analysis.T, logw.reshape(width), ess.reshape(())


def solve_blocks(moment, target):
    factor = jnp.linalg.cholesky(moment)
    return jax.vmap(lambda lower, right: jax.scipy.linalg.cho_solve((lower, True), right))(
        factor, target
    )


def reduced_shards(ensemble, obs_values, obs_sigma, obs_operator, block_cols, batch_order):
    block_size = obs_operator.shape[-1]
    row_count, mem_dev = ensemble.shape
    nblocks = row_count // block_size
    members = mem_dev * lax.axis_size("mem")
    batches, obs_blocks, col_count = block_cols.shape
    temper = 1.0 / math.sqrt(batches * obs_blocks * block_size)
    offset = lax.axis_index("st") * nblocks
    states = ensemble.reshape(nblocks, block_size, mem_dev)
    eye = jnp.eye(block_size, dtype=jnp.float32)
    slots = jnp.arange(nblocks, dtype=jnp.int32)
    loglik = jnp.zeros((mem_dev,), jnp.float32)
    for batch_step in range(batches):
        chosen = batch_order[batch_step]
        operator_now = lax.dynamic_index_in_dim(obs_operator, chosen, 0, keepdims=False)
        columns = lax.dynamic_index_in_dim(block_cols, chosen, 0, keepdims=False)
        values_now = lax.dynamic_index_in_dim(obs_values, chosen, 0, keepdims=False)
        sigma_now = lax.dynamic_index_in_dim(obs_sigma, chosen, 0, keepdims=False)
        local_ids = columns.reshape(-1) - offset
        selector = (local_ids[:, None] == slots[None, :]).astype(jnp.float32)
        picked = jnp.einsum("ps,sim->pim", selector, states, precision=precise)
        picked = picked.reshape(obs_blocks, col_count, block_size, mem_dev)
        partial_value = jnp.einsum("bkij,bkjm->bim", operator_now, picked, precision=precise)
        image = lax.psum(partial_value, "st")
        misfit = (values_now[:, :, None] - image) / sigma_now[:, :, None]
        loglik = loglik - 0.5 * temper * jnp.sum(misfit * misfit, axis=(0, 1))
        center = lax.psum(jnp.sum(image, axis=2), "mem") / members
        anomaly = image - center[:, :, None]
        moment_sum, cross_sum = lax.psum(
            (
                jnp.einsum("bim,bjm->bij", anomaly, anomaly, precision=precise),
                jnp.einsum("bkim,bjm->bkij", picked, anomaly, precision=precise),
            ),
            "mem",
        )
        moment = moment_sum / (members - 1) + eye * (sigma_now * sigma_now)[:, :, None]
        cross = cross_sum / (members - 1)
        target = (values_now - center)[:, :, None] - 0.5 * anomaly
        weights = solve_blocks(moment, target)
        change = jnp.einsum("bkij,bjm->bkim", cross, weights, precision=precise)
        change = change.reshape(obs_blocks * col_count, block_size, mem_dev)
        states = states + jnp.einsum("ps,pim->sim", selector, change, precision=precise)
    largest_local = jnp.max(loglik)
    largest = lax.pmax(largest_local, "mem")
    scaled = jnp.exp(loglik - largest)
    summed, squares = lax.psum((jnp.sum(scaled), jnp.sum(scaled * scaled)), "mem")
    log_weights = loglik - largest - jnp.log(summed)
    ess = summed * summed / squares
    return (states.reshape(row_count, mem_dev), log_weights, ess)


def shards(ensemble, *others):
    devices = lax.axis_size("mem") * lax.axis_size("st")
    fits = 4 * ensemble.size * devices <= GATHER_LIMIT
    return (gathered_shards if fits else reduced_shards)(ensemble, *others)


def solution(mesh):
    placed = (P("st", "mem"), P(), P(), P(), P(), P())
    return jax.shard_map(
        shards,
        mesh=mesh,
        in_specs=placed,
        out_specs=(P("st", "mem"), P("mem"), P()),
        check_vma=False,
    )
```

```python
import functools
import math

import jax
import jax.numpy as jnp
from jax import lax
from jax.experimental import pallas as pl
from jax.experimental.pallas import tpu as pltpu
from jax.sharding import PartitionSpec as P

precise = lax.Precision.HIGHEST
PANEL = 16
SUB = 8
GATHER_LIMIT = 16 << 20
CUTS = 2
REACH = 1


def halves(x):
    high = x.astype(jnp.bfloat16)
    return high, (x - high.astype(jnp.float32)).astype(jnp.bfloat16)


def thirds(x):
    high = x.astype(jnp.bfloat16)
    rest = x - high.astype(jnp.float32)
    mid = rest.astype(jnp.bfloat16)
    return high, mid, (rest - mid.astype(jnp.float32)).astype(jnp.bfloat16)


def mul_nn(a, b):
    return lax.dot_general(a, b, (((1,), (0,)), ((), ())), preferred_element_type=jnp.float32)


def mul_nt(a, b):
    return lax.dot_general(a, b, (((1,), (1,)), ((), ())), preferred_element_type=jnp.float32)


def factor(moments, crossed, obs_blocks, size):
    lanes = lax.broadcasted_iota(jnp.int32, (obs_blocks, size), 1)
    own = lanes % obs_blocks == lax.broadcasted_iota(jnp.int32, (obs_blocks, size), 0)
    own = own.astype(jnp.float32)[:, : PANEL * obs_blocks]

    def spread(rows, lane):
        count = len(rows)
        tall = jnp.concatenate(rows, axis=0)
        tall = jnp.broadcast_to(tall[:, lane : lane + 1], (count * obs_blocks, size))
        return [tall[r * obs_blocks : (r + 1) * obs_blocks] for r in range(count)]

    def line(r):
        return slice(r * obs_blocks, (r + 1) * obs_blocks)

    def updates(rhs, low, high):
        parts = []
        for k in range(3):
            wide = [jnp.broadcast_to(crossed[k, r : r + 1, :], own.shape) * own for r in range(low, high)]
            parts.append(jnp.concatenate(wide, axis=0).astype(jnp.bfloat16))
        main = mul_nn(jnp.concatenate([parts[0], parts[1]], axis=1), rhs[0])
        return main[:, size:] + mul_nn(jnp.concatenate([parts[2], parts[0]], axis=1), rhs[1]) + main[:, :size]

    rows = [moments[line(i), :] for i in range(PANEL)]
    pending = []
    for first in range(0, size, PANEL):
        for sub in range(0, PANEL, SUB):
            base = first + sub
            inside = (lanes >= base) & (lanes < base + SUB)
            entry = {}
            for j in range(SUB):
                for i, value in zip(range(j, SUB), spread(rows[sub + j : sub + SUB], base + j)):
                    entry[i, j] = value
            while pending:
                pending.pop()()
            for i in range(SUB):
                rows[sub + i] = jnp.where(inside, (lanes == base + i).astype(jnp.float32), rows[sub + i])
            for p in range(SUB):
                root = lax.rsqrt(entry[p, p])
                rows[sub + p] = rows[sub + p] * root
                column = {i: entry[i, p] * root for i in range(p + 1, SUB)}
                for i in range(p + 1, SUB):
                    for j in range(p + 1, i + 1):
                        entry[i, j] = entry[i, j] - column[i] * column[j]
                for i in range(p + 1, SUB):
                    rows[sub + i] = rows[sub + i] - column[i] * rows[sub + p]
            for i in range(sub + SUB, PANEL):
                row = jnp.where(inside, 0.0, rows[i])
                for p, value in zip(range(sub, sub + SUB), spread(rows[sub : sub + SUB], first + i)):
                    row = row - value * rows[p]
                rows[i] = row
        for i in range(PANEL - SUB):
            later = first + i // SUB * SUB + SUB
            rows[i] = jnp.where((lanes >= later) & (lanes < first + PANEL), 0.0, rows[i])
        for i in range(PANEL):
            moments[line(first + i), :] = rows[i]
        below = first + PANEL
        if below == size:
            return
        stack = jnp.concatenate(rows, axis=0)
        high, mid, low = thirds(stack)
        across = thirds(stack.T)
        for k in range(3):
            crossed[k, :, :] = across[k].astype(jnp.float32)
        rhs = [
            jnp.concatenate([jnp.concatenate([high, mid], axis=1)] * 2, axis=0),
            jnp.concatenate([high, low], axis=0),
        ]
        inside = (lanes >= first) & (lanes < below)
        change = updates(rhs, below, below + PANEL)
        rows = [jnp.where(inside, 0.0, moments[line(below + i), :]) - change[line(i)] for i in range(PANEL)]
        if below + PANEL < size:
            def later(rhs=rhs, inside=inside, low=below + PANEL):
                change = updates(rhs, low, size)
                for i in range(size - low):
                    here = line(low + i)
                    moments[here, :] = jnp.where(inside, 0.0, moments[here, :]) - change[line(i)]
            pending.append(later)


def kernel(
    members, order, columns, place, values, sigma, operator, gathered,
    states, analysis, logw, ess,
    picks, parts, moments, crossed, misfits, whites, targets, crosses,
):
    batches, obs_blocks, size = values.shape
    _, width, row_count = states.shape
    mem_count = members // width
    blocks = row_count // size
    misfits[...] = jnp.zeros_like(misfits)
    line = lax.broadcasted_iota(jnp.int32, (size, size), 0)
    cols = lax.broadcasted_iota(jnp.int32, (size, size), 1)
    eye = (line == cols).astype(jnp.float32)
    below_diagonal = line >= cols

    def spot(block):
        level = pl.ds((block // blocks) * mem_count, mem_count)
        return level, slice(None), pl.ds(pl.multiple_of((block % blocks) * size, size), size)

    @pl.loop(0, batches)
    def _(step):
        chosen = order[step]
        values_now, sigma_now = values[chosen], sigma[chosen]
        values_t, sigma_t = values_now.T, sigma_now.T
        centers = []
        for b in range(obs_blocks):
            sides = []
            for k in range(2):
                sides.append(states[spot(columns[chosen, k, b])].reshape(members, size))
            high, mid = halves(jnp.concatenate(sides, axis=1))
            picks[b, 0] = high
            picks[b, 1] = mid
            h_high, h_mid = halves(jnp.concatenate([operator[chosen, b, 0], operator[chosen, b, 1]], axis=1))
            image = mul_nt(jnp.concatenate([h_high, h_mid], axis=0), high)
            image = image[:size] + image[size:] + mul_nt(h_high, mid)
            value, deviation = values_t[:, b : b + 1], sigma_t[:, b : b + 1]
            misfit = (value - image) * (1.0 / deviation)
            misfits[...] += jnp.sum((misfit * misfit).reshape(size // 8, 8, members), axis=0)
            center = jnp.sum(image, axis=1, keepdims=True) * (1.0 / members)
            centers.append(center)
            high, mid, low = thirds(image - center)
            tall = jnp.concatenate([high, mid, low], axis=0)
            parts[b] = tall
        for b in range(obs_blocks):
            tall = parts[b]
            deviation = sigma_t[:, b : b + 1]
            product = mul_nt(tall, tall[: 2 * size])
            cross = product[:size, size:] + product[2 * size :, :size]
            total = (product[size : 2 * size, size:] + (cross + cross.T)) + product[:size, :size]
            moments[pl.ds(b, size, stride=obs_blocks), :] = total * (1.0 / (members - 1)) + eye * (deviation * deviation)
        offsets = values_now - jnp.concatenate(centers, axis=1).T

        factor(moments, crossed, obs_blocks, size)

        for b in range(obs_blocks):
            lower = jnp.where(below_diagonal, moments[pl.ds(b, size, stride=obs_blocks), :], 0.0)
            shift = jnp.sum(lower * offsets[b : b + 1, :], axis=1, keepdims=True)
            l_high, l_mid, l_low = thirds(lower)
            tall = parts[b]
            pair = jnp.concatenate([jnp.concatenate([l_high, l_high], axis=1), jnp.concatenate([l_mid, l_mid], axis=1)], axis=0)
            first = mul_nn(pair, tall[: 2 * size])
            last = mul_nn(jnp.concatenate([l_low, l_high], axis=1), jnp.concatenate([tall[:size], tall[2 * size :]], axis=0))
            whitened = first[:size] + (first[size:] + last)
            whites[b] = jnp.concatenate(halves(whitened), axis=0)
            targets[b] = (shift - 0.5 * whitened) * (1.0 / (members - 1))
        for b in range(obs_blocks):
            cross = mul_nn(whites[b], picks[b, 0])
            cross = cross[:size] + cross[size:] + mul_nn(whites[b, :size], picks[b, 1])
            crosses[b] = jnp.concatenate(halves(cross), axis=0)
        for b in range(obs_blocks):
            t_high, t_mid = halves(targets[b].T)
            change = mul_nn(jnp.concatenate([t_high, t_high], axis=1), crosses[b])
            change = change + mul_nn(t_mid, crosses[b, :size])
            for k in range(2):
                where = spot(columns[chosen, k, b])
                states[where] += change[:, k * size : (k + 1) * size].reshape(mem_count, width, size)

    temper = 1.0 / math.sqrt(batches * obs_blocks * size)
    likely = -0.5 * temper * jnp.sum(misfits[...], axis=0, keepdims=True)
    largest = jnp.max(likely, axis=1, keepdims=True)
    scaled = jnp.exp(likely - largest)
    summed = jnp.sum(scaled, axis=1, keepdims=True)
    squares = jnp.sum(scaled * scaled, axis=1, keepdims=True)
    ess[...] = summed * summed / squares
    logs = jnp.broadcast_to(likely - largest - jnp.log(summed), (8, members))
    logs = pltpu.roll(logs, lax.rem(members - place[0] * width, members), 1)
    logw[...] = logs[:1, :width]
    analysis[...] = states[place[1] * mem_count + place[0]]


MESH = pl.DeviceIdType.MESH


def gather_kernel(piece, gathered, send_sems, recv_sems, local_sem):
    me, z = lax.axis_index("mem"), lax.axis_index("st")
    depth, width = lax.axis_size("st"), lax.axis_size("mem")
    core, bit = me % 2, (me // 2) % 2
    twin = me + 1 - 2 * core
    flat = me + 2 - 4 * bit
    upright = (me + width // 2) % width
    corner = (flat + width // 2) % width
    kinds = {"up": 0, "down": 1, "flat": 2, "upright": 3, "twin": 4}
    targets = {"up": (me, z + 1), "down": (me, z - 1), "flat": (flat, z), "upright": (upright, z), "twin": (twin, z)}
    share = piece.shape[0] // CUTS

    def copy(kind, slot, cut, source=None):
        rows = pl.ds(cut * share, share)
        here = gathered.at[slot, rows]
        return pltpu.make_async_remote_copy(
            src_ref=here if source is None else source.at[rows],
            dst_ref=here,
            send_sem=send_sems.at[(kinds[kind] * depth * width + slot) * CUTS + cut],
            recv_sem=recv_sems.at[slot * CUTS + cut],
            device_id=targets[kind],
            device_id_type=MESH,
        )

    def arrive(slot, cut):
        copy("twin", slot, cut).wait_recv()

    barrier = pltpu.get_barrier_semaphore()
    for kind in ("flat", "upright", "twin"):
        pl.semaphore_signal(barrier, inc=1, device_id=targets[kind], device_id_type=MESH)

    @pl.when(z < depth - 1)
    def _():
        pl.semaphore_signal(barrier, inc=1, device_id=targets["up"], device_id_type=MESH)

    @pl.when(z > 0)
    def _():
        pl.semaphore_signal(barrier, inc=1, device_id=targets["down"], device_id_type=MESH)

    @pl.when((z > 0) & (z < depth - 1))
    def _():
        pl.semaphore_wait(barrier, 5)

    @pl.when((z == 0) | (z == depth - 1))
    def _():
        pl.semaphore_wait(barrier, 4)

    def along(action, slot, cut, distance, rising, source=None):
        if distance == 0 or rising:
            @pl.when(z < depth - 1)
            def _():
                action(copy("up", slot, cut, source))

        if distance == 0 or not rising:
            @pl.when(z > 0)
            def _():
                action(copy("down", slot, cut, source))

    def column(action, level, cut, distance, rising, wait):
        slot = level * width + me
        source = piece if distance == 0 else None
        if wait:
            arrive(slot, cut)
        along(action, slot, cut, distance, rising, source)
        for kind in ("flat", "upright", "twin"):
            action(copy(kind, slot, cut, source))

    def plane(action, level, cut, distance, rising, wait):
        for first, onward, parity in ((flat, "upright", 1), (upright, "flat", 0)):
            slot = level * width + first
            if wait:
                arrive(slot, cut)
            if distance == 0 or distance > REACH + 1 - cut:
                @pl.when((level + cut) % 2 == parity)
                def _():
                    action(copy(onward, slot, cut))

            action(copy("twin", slot, cut))

    def far(action, level, cut, distance, rising, wait):
        slot = level * width + corner
        if wait:
            arrive(slot, cut)
        if distance < REACH + 1 - cut:
            along(action, slot, cut, distance, rising)
        action(copy("twin", slot, cut))

    def around(distance, do):
        if distance == 0:
            do(z, True)
            return

        @pl.when(z >= distance)
        def _():
            do(z - distance, True)

        @pl.when(z + distance < depth)
        def _():
            do(z + distance, False)

    def start(descriptor):
        descriptor.start()

    def finish(descriptor):
        descriptor.wait_send()

    own = pltpu.make_async_copy(piece, gathered.at[z * width + me], local_sem)
    own.start()

    for turn in range(0, depth + 2):
        for part, late in ((column, 0), (plane, 1), (far, 2)):
            distance = turn - late
            if 0 <= distance < depth:
                def go(level, rising, part=part, distance=distance):
                    for cut in range(CUTS):
                        part(start, level, cut, distance, rising, not (part is column and distance == 0))
                around(distance, go)
    for distance in range(depth):
        def rest(level, rising, distance=distance):
            for cut in range(CUTS):
                for other in (twin, flat + twin - me, upright + twin - me, corner + twin - me):
                    arrive(level * width + other, cut)
                for part in (column, plane, far):
                    part(finish, level, cut, distance, rising, False)
        around(distance, rest)
    own.wait()


def gather_all(piece):
    depth, width = lax.axis_size("st"), lax.axis_size("mem")
    if width != 8 or depth < 2:
        return lax.all_gather(piece, ("st", "mem"))
    return pl.pallas_call(
        gather_kernel,
        out_shape=jax.ShapeDtypeStruct((depth * width, *piece.shape), piece.dtype),
        in_specs=[pl.BlockSpec(memory_space=pl.ANY)],
        out_specs=pl.BlockSpec(memory_space=pltpu.VMEM),
        scratch_shapes=[
            pltpu.SemaphoreType.DMA((5 * depth * width * CUTS,)),
            pltpu.SemaphoreType.DMA((depth * width * CUTS,)),
            pltpu.SemaphoreType.DMA,
        ],
        compiler_params=pltpu.CompilerParams(collective_id=0, has_side_effects=True, vmem_limit_bytes=GATHER_LIMIT),
    )(piece)


def gathered_shards(ensemble, obs_values, obs_sigma, obs_operator, block_cols, batch_order):
    size = obs_operator.shape[-1]
    row_count, width = ensemble.shape
    blocks = row_count // size
    mem_count, st_count = lax.axis_size("mem"), lax.axis_size("st")
    members = width * mem_count
    batches, obs_blocks, _ = block_cols.shape
    gathered = gather_all(ensemble.T)
    place = jnp.stack([lax.axis_index("mem"), lax.axis_index("st")]).astype(jnp.int32)
    smem = pl.BlockSpec(memory_space=pltpu.SMEM)
    vmem = pl.BlockSpec(memory_space=pltpu.VMEM)
    _, analysis, logw, ess = pl.pallas_call(
        functools.partial(kernel, members),
        out_shape=(
            jax.ShapeDtypeStruct(gathered.shape, jnp.float32),
            jax.ShapeDtypeStruct((width, row_count), jnp.float32),
            jax.ShapeDtypeStruct((1, width), jnp.float32),
            jax.ShapeDtypeStruct((1, 1), jnp.float32),
        ),
        in_specs=[smem, smem, smem, vmem, vmem, vmem, vmem],
        out_specs=(vmem, vmem, vmem, vmem),
        input_output_aliases={6: 0},
        scratch_shapes=[
            pltpu.VMEM((obs_blocks, 2, members, 2 * size), jnp.bfloat16),
            pltpu.VMEM((obs_blocks, 3 * size, members), jnp.bfloat16),
            pltpu.VMEM((size * obs_blocks, size), jnp.float32),
            pltpu.VMEM((3, size, PANEL * obs_blocks), jnp.float32),
            pltpu.VMEM((8, members), jnp.float32),
            pltpu.VMEM((obs_blocks, 2 * size, members), jnp.bfloat16),
            pltpu.VMEM((obs_blocks, size, members), jnp.float32),
            pltpu.VMEM((obs_blocks, 2 * size, 2 * size), jnp.bfloat16),
        ],
        compiler_params=pltpu.CompilerParams(vmem_limit_bytes=32 << 20),
    )(batch_order, block_cols.transpose(0, 2, 1), place, obs_values, obs_sigma, obs_operator, gathered)
    return analysis.T, logw.reshape(width), ess.reshape(())


def solve_blocks(moment, target):
    factor = jnp.linalg.cholesky(moment)
    return jax.vmap(lambda lower, right: jax.scipy.linalg.cho_solve((lower, True), right))(
        factor, target
    )


def reduced_shards(ensemble, obs_values, obs_sigma, obs_operator, block_cols, batch_order):
    block_size = obs_operator.shape[-1]
    row_count, mem_dev = ensemble.shape
    nblocks = row_count // block_size
    members = mem_dev * lax.axis_size("mem")
    batches, obs_blocks, col_count = block_cols.shape
    temper = 1.0 / math.sqrt(batches * obs_blocks * block_size)
    offset = lax.axis_index("st") * nblocks
    states = ensemble.reshape(nblocks, block_size, mem_dev)
    eye = jnp.eye(block_size, dtype=jnp.float32)
    slots = jnp.arange(nblocks, dtype=jnp.int32)
    loglik = jnp.zeros((mem_dev,), jnp.float32)
    for batch_step in range(batches):
        chosen = batch_order[batch_step]
        operator_now = lax.dynamic_index_in_dim(obs_operator, chosen, 0, keepdims=False)
        columns = lax.dynamic_index_in_dim(block_cols, chosen, 0, keepdims=False)
        values_now = lax.dynamic_index_in_dim(obs_values, chosen, 0, keepdims=False)
        sigma_now = lax.dynamic_index_in_dim(obs_sigma, chosen, 0, keepdims=False)
        local_ids = columns.reshape(-1) - offset
        selector = (local_ids[:, None] == slots[None, :]).astype(jnp.float32)
        picked = jnp.einsum("ps,sim->pim", selector, states, precision=precise)
        picked = picked.reshape(obs_blocks, col_count, block_size, mem_dev)
        partial_value = jnp.einsum("bkij,bkjm->bim", operator_now, picked, precision=precise)
        image = lax.psum(partial_value, "st")
        misfit = (values_now[:, :, None] - image) / sigma_now[:, :, None]
        loglik = loglik - 0.5 * temper * jnp.sum(misfit * misfit, axis=(0, 1))
        center = lax.psum(jnp.sum(image, axis=2), "mem") / members
        anomaly = image - center[:, :, None]
        moment_sum, cross_sum = lax.psum(
            (
                jnp.einsum("bim,bjm->bij", anomaly, anomaly, precision=precise),
                jnp.einsum("bkim,bjm->bkij", picked, anomaly, precision=precise),
            ),
            "mem",
        )
        moment = moment_sum / (members - 1) + eye * (sigma_now * sigma_now)[:, :, None]
        cross = cross_sum / (members - 1)
        target = (values_now - center)[:, :, None] - 0.5 * anomaly
        weights = solve_blocks(moment, target)
        change = jnp.einsum("bkij,bjm->bkim", cross, weights, precision=precise)
        change = change.reshape(obs_blocks * col_count, block_size, mem_dev)
        states = states + jnp.einsum("ps,pim->sim", selector, change, precision=precise)
    largest_local = jnp.max(loglik)
    largest = lax.pmax(largest_local, "mem")
    scaled = jnp.exp(loglik - largest)
    summed, squares = lax.psum((jnp.sum(scaled), jnp.sum(scaled * scaled)), "mem")
    log_weights = loglik - largest - jnp.log(summed)
    ess = summed * summed / squares
    return (states.reshape(row_count, mem_dev), log_weights, ess)


def shards(ensemble, *others):
    devices = lax.axis_size("mem") * lax.axis_size("st")
    fits = 4 * ensemble.size * devices <= GATHER_LIMIT
    return (gathered_shards if fits else reduced_shards)(ensemble, *others)


def solution(mesh):
    placed = (P("st", "mem"), P(), P(), P(), P(), P())
    return jax.shard_map(
        shards,
        mesh=mesh,
        in_specs=placed,
        out_specs=(P("st", "mem"), P("mem"), P()),
        check_vma=False,
    )
```
